32 devices in a mesh: seq: 16 (over z, y, x), chan: 2 (over core).
Axes of the slice: x: 2, y: 2, z: 4, core: 2. Of those that a mesh axis runs over, the one named last changes fastest.
Arguments:
- tokens: bfloat16 [32768, 1024], P('seq', 'chan'), may hold values from -30 to 30, as said below
- cotangent: bfloat16 [32768, 1024], P('seq', 'chan'), may hold values from -12 to 12, as said below
- norm_gain: float32 [1024], P('chan'), may hold values from 0.5 to 1.5
- gate_slope: float32 [1024], P('chan'), may hold values from -3 to 3
- gate_bias: float32 [1024], P('chan'), may hold values from -1 to 1
- right_factor: bfloat16 [512, 512], P('chan'), may hold values from -0.25 to 0.25
- left_factor: bfloat16 [64, 64], P('chan'), may hold values from -0.75 to 0.75
- twiddle: float32 [64, 512], P('seq'), may hold values from -4 to 4
Outputs:
- mixed: bfloat16 [32768, 1024], P('seq', 'chan')
- token_grad: bfloat16 [32768, 1024], P('seq', 'chan')
- right_grad: float32 [512, 512], P('seq', 'chan')
- left_grad: float32 [64, 64], P('seq', 'chan')
- twiddle_grad: float32 [64, 512], P('seq')
- gain_grad: float32 [1024], P('chan')
- slope_grad: float32 [1024], P('chan')
- bias_grad: float32 [1024], P('chan')
The draws below stay inside these ranges and needn't reach their ends.
Inputs may be any that keep to these rules, and one draw needn't show every extreme that they name: `tokens`: Real-valued activations of varying scale. `cotangent`: Real-valued cotangents.
All inputs are finite; a program needn't handle non-finite values.
Results may differ from the reference program's by a relative error of at most 0.0069.
Values may be sent and summed in bfloat16 or wider, within the bound.
No kernel may reach another device: no remote copies, remote signals or barrier semaphores. Data moves between devices by JAX's collectives and lax.ppermute only.
A program may use at most 128 MiB of HBM per device.

```python
import math
import jax
import jax.numpy as jnp
from jax import lax

D = 1024
B = 512
A = 64
LENGTH = 32768
N_CHAN = 2


def draw_tokens(key, part):
    key_list = jax.random.split(key, 3)
    full_shape = (LENGTH, D)
    entries = jax.random.truncated_normal(key_list[0], -4.0, 4.0, full_shape, jnp.float32)
    row_scales = jnp.exp(jax.random.uniform(key_list[1], (LENGTH, 1), jnp.float32, -0.5 * math.log(10.0), 0.5 * math.log(10.0)))
    channel_ramp = jnp.arange(D, dtype=jnp.float32) / D - 0.5
    col_scales = jnp.exp(math.log(3.0) * channel_ramp + jax.random.uniform(key_list[2], (D,), jnp.float32, -0.3, 0.3))
    return (entries * row_scales * col_scales[None, :]).astype(jnp.bfloat16)


def draw_cotangent(key, part):
    key_list = jax.random.split(key, 1)
    full_shape = (LENGTH, D)
    entries = jax.random.truncated_normal(key_list[0], -4.0, 4.0, full_shape, jnp.float32)
    position_ramp = jnp.arange(LENGTH, dtype=jnp.float32) / LENGTH - 0.5
    channel_ramp = jnp.arange(D, dtype=jnp.float32) / D - 0.5
    scales = jnp.exp(math.log(3.0) * (position_ramp[:, None] + channel_ramp[None, :]))
    return (entries * scales).astype(jnp.bfloat16)


def block_levels(rng, shape, cuts, low, high):
    gain, own = 1.0, jax.random.fold_in(rng, 6)
    for position, shards_of in cuts:
        draws = jnp.exp(jax.random.uniform(jax.random.fold_in(own, position), (shards_of,), jnp.float32, low / len(cuts), high / len(cuts)))
        gain = gain * jnp.repeat(draws, shape[position] // shards_of).reshape([-1 if axis == position else 1 for axis in range(len(shape))])
    return gain


def gaussian(rng, shape, scale, reach, cuts=(), kind=jnp.bfloat16):
    drawn = jax.random.normal(rng, shape, jnp.float32) * scale
    if len(cuts) > 0:
        drawn = block_levels(rng, shape, cuts, -0.22, 0.18) * drawn
    return jnp.clip(drawn, min=-reach, max=reach).astype(kind)


def setup_inputs(seed: int = 0) -> dict:
    arg_keys = jax.random.split(jax.random.key(seed), 9)
    tokens = draw_tokens(jax.random.fold_in(arg_keys[8], 71), 0)
    cotangent = draw_cotangent(jax.random.fold_in(arg_keys[8], 71), 0)
    norm_gain = jnp.clip(1.0 + 0.1 * jax.random.normal(arg_keys[2], (D,), jnp.float32), 0.5, 1.5)
    gate_slope = gaussian(arg_keys[3], (D,), 1.0, 3.0, ((0, 2),), jnp.float32)
    gate_bias = jnp.clip(jax.random.uniform(arg_keys[4], (D,), jnp.float32, -1.0, 1.0) * block_levels(arg_keys[4], (D,), ((0, 2),), -0.4, 0.0), -1.0, 1.0)
    right_factor = gaussian(arg_keys[5], (B, B), B ** -0.5, 0.25, ((0, 2),))
    left_factor = gaussian(arg_keys[6], (A, A), A ** -0.5, 0.75, ((0, 2),))
    twiddle = gaussian(arg_keys[7], (A, B), 1.0, 4.0, ((0, 16),), jnp.float32)
    return {"tokens": tokens, "cotangent": cotangent, "norm_gain": norm_gain, "gate_slope": gate_slope, "gate_bias": gate_bias, "right_factor": right_factor, "left_factor": left_factor, "twiddle": twiddle}


def split_channels(array):
    chan_width = D // N_CHAN
    return array.reshape(A, B, N_CHAN, chan_width).transpose(2, 0, 1, 3)

def join_channels(array):
    return array.transpose(1, 2, 0, 3).reshape(A * B, D)

def reference(tokens, cotangent, norm_gain, gate_slope, gate_bias, right_factor, left_factor, twiddle):
    chan_width = D // N_CHAN
    wide_tokens = tokens.astype(jnp.float32)
    row_scale = lax.rsqrt(lax.optimization_barrier(jnp.sum(wide_tokens * wide_tokens, axis=1)) / D + 1e-05)
    scale_grid = row_scale.reshape(A, B, 1)
    right_wide = right_factor.astype(jnp.float32)
    left_wide = left_factor.astype(jnp.float32)
    twiddle_grid = twiddle[:, :, None]

    def one_block(totals, pieces):
        right_grad, left_grad, twiddle_grad = totals
        token_part, cot_part, gain_part, slope_part, bias_part = pieces
        token_part = token_part.astype(jnp.float32)
        cot_part = cot_part.astype(jnp.float32)
        normed = token_part * scale_grid * gain_part
        normed_b = lax.optimization_barrier(normed.astype(jnp.bfloat16)).astype(jnp.float32)
        gate_value = jax.nn.sigmoid(slope_part * normed + bias_part)
        first_mix = jnp.einsum('ij,ajc->aic', right_wide, normed_b)
        spread = lax.optimization_barrier((first_mix * twiddle_grid).astype(jnp.bfloat16)).astype(jnp.float32)
        second_mix = jnp.einsum('ja,aic->jic', left_wide, spread)
        second_mix = lax.optimization_barrier(second_mix.astype(jnp.bfloat16)).astype(jnp.float32)
        mixed_part = (gate_value * second_mix).astype(jnp.bfloat16)
        cot_gated = lax.optimization_barrier((cot_part * gate_value).astype(jnp.bfloat16)).astype(jnp.float32)
        gate_grad = cot_part * second_mix * gate_value * (1.0 - gate_value)
        left_grad = left_grad + jnp.einsum('jic,aic->ja', cot_gated, spread)
        spread_grad = jnp.einsum('ja,jic->aic', left_wide, cot_gated)
        spread_grad = lax.optimization_barrier(spread_grad.astype(jnp.bfloat16)).astype(jnp.float32)
        twiddle_grad = twiddle_grad + lax.optimization_barrier(jnp.sum(spread_grad * first_mix, axis=2))
        first_grad = lax.optimization_barrier((spread_grad * twiddle_grid).astype(jnp.bfloat16)).astype(jnp.float32)
        right_grad = right_grad + jnp.einsum('aic,abc->ib', first_grad, normed_b)
        normed_grad = jnp.einsum('ib,aic->abc', right_wide, first_grad) + gate_grad * slope_part
        scaled_grad = normed_grad * gain_part
        gain_grad = lax.optimization_barrier(jnp.sum(normed_grad * token_part * scale_grid, axis=(0, 1)))
        slope_grad = lax.optimization_barrier(jnp.sum(gate_grad * normed, axis=(0, 1)))
        bias_grad = lax.optimization_barrier(jnp.sum(gate_grad, axis=(0, 1)))
        return ((right_grad, left_grad, twiddle_grad), (mixed_part, scaled_grad, gain_grad, slope_grad, bias_grad))
    pieces = (split_channels(tokens), split_channels(cotangent), norm_gain.reshape(N_CHAN, chan_width), gate_slope.reshape(N_CHAN, chan_width), gate_bias.reshape(N_CHAN, chan_width))
    start = (jnp.zeros((B, B), jnp.float32), jnp.zeros((A, A), jnp.float32), jnp.zeros((A, B), jnp.float32))
    totals, stacked = lax.scan(one_block, start, pieces)
    right_grad, left_grad, twiddle_grad = totals
    mixed_parts, scaled_parts, gain_grad, slope_grad, bias_grad = stacked
    mixed = join_channels(mixed_parts)
    scaled_grad = join_channels(scaled_parts)
    inner_sum = lax.optimization_barrier(jnp.sum(scaled_grad * wide_tokens, axis=1))
    token_grad = (row_scale[:, None] * scaled_grad - wide_tokens * (row_scale ** 3)[:, None] * inner_sum[:, None] / D).astype(jnp.bfloat16)
    return (mixed, token_grad, right_grad, left_grad, twiddle_grad, gain_grad.reshape(D), slope_grad.reshape(D), bias_grad.reshape(D))
```

```python
import functools

import jax
import jax.numpy as jnp
from jax import lax
from jax.experimental import pallas as pl
from jax.experimental.pallas import tpu as pltpu
from jax.sharding import PartitionSpec as P

D = 1024
B = 512
EPS = 1e-05
LAG = 8

F32 = jnp.float32
BF16 = jnp.bfloat16


def sds(shape, dtype):
    return jax.ShapeDtypeStruct(shape, dtype)


def cost(flops, nbytes):
    return pl.CostEstimate(flops=int(flops), bytes_accessed=int(nbytes), transcendentals=0)


def params():
    return pltpu.CompilerParams(vmem_limit_bytes=56 * 1024 * 1024)


def whole(shape):
    zeros = (0,) * len(shape)
    return pl.BlockSpec(shape, lambda *_: zeros)


def partners(n, sign):
    me = lax.axis_index("seq")
    hi, lo = me // 4, me % 4
    high = n // 4
    lo_of = [lo, lo + 1 - 2 * (lo % 2), (lo + 2) % 4, 3 - lo]
    return [
        ((hi + (sign * (k // 4)) % high) % high) * 4 + lo_of[k % 4]
        for k in range(n)
    ]


def pairs(n, k):
    high = n // 4
    return [
        (i, ((i // 4 + k // 4) % high) * 4 + ((i % 4) ^ (k % 4)))
        for i in range(n)
    ]


def send_order(n):
    high = n // 4
    far_first = sorted(range(1, high), key=lambda d: (abs(d - high / 2), d))
    order = []
    for dl in range(4):
        order += [4 * dh + dl for dh in far_first]
        if dl < 3:
            order.append(dl + 1)
    return order


def exchange(blocks):
    n = len(blocks)
    out = list(blocks)
    for k in send_order(n):
        out[k] = lax.ppermute(blocks[k], "seq", pairs(n, k))
    return out


def after_part(values, started):
    keys = send_order(len(started))[:LAG]
    values, held = lax.optimization_barrier((values, [started[k] for k in keys]))
    started = list(started)
    for k, v in zip(keys, held):
        started[k] = v
    return values, started


def chan_terms(x):
    nc = lax.axis_size("chan")
    if nc == 2:
        return x, lax.ppermute(x, "chan", [(0, 1), (1, 0)])
    return lax.psum(x, "chan"), jnp.zeros_like(x)


def chan_gather(x):
    nc = lax.axis_size("chan")
    if nc != 2:
        return lax.all_gather(x, "chan", axis=0, tiled=True)
    other = lax.ppermute(x, "chan", [(0, 1), (1, 0)])
    first = lax.axis_index("chan") == 0
    return jnp.concatenate(
        [jnp.where(first, x, other), jnp.where(first, other, x)], axis=0
    )


def chan_scatter(x):
    nc = lax.axis_size("chan")
    if nc != 2:
        return lax.psum_scatter(x, "chan", scatter_dimension=x.ndim - 1, tiled=True)
    half = x.shape[-1] // 2
    first = lax.axis_index("chan") == 0
    low, high = x[..., :half], x[..., half:]
    other = lax.ppermute(jnp.where(first, high, low), "chan", [(0, 1), (1, 0)])
    return jnp.where(first, low, high) + other


def row_sums(x):
    high = x.astype(BF16)
    low = (x - high.astype(F32)).astype(BF16)
    ones = jnp.ones((8, x.shape[1]), BF16)
    dims = (((1,), (1,)), ((), ()))
    return lax.dot_general(ones, high, dims, preferred_element_type=F32) + lax.dot_general(
        ones, low, dims, preferred_element_type=F32
    )


def column(rows):
    return rows.T[:, :1]


def scale_of(sa_ref, sb_ref):
    return column(lax.rsqrt((sa_ref[...] + sb_ref[...]) / D + EPS))


sigmoid = jax.nn.sigmoid


def squares_kernel(tok_ref, out_ref):
    x = tok_ref[...].astype(F32)
    out_ref[...] = row_sums(x * x)


def squares(tokens):
    rows, width = tokens.shape
    return pl.pallas_call(
        squares_kernel,
        grid=(rows // B,),
        in_specs=[pl.BlockSpec((B, width), lambda a: (a, 0))],
        out_specs=pl.BlockSpec((8, B), lambda a: (0, a)),
        out_shape=sds((8, rows), F32),
        compiler_params=params(),
        cost_estimate=cost(8 * rows * width, 2 * rows * width),
        name="squares",
    )(tokens)


def gate_kernel(n, tok_ref, cot_ref, sa_ref, sb_ref, gain_ref, slope_ref, bias_ref, *rest):
    nb_ref, outs, held = rest[0], rest[1 : 1 + n], rest[1 + n]
    size = B // n
    normed = tok_ref[...].astype(F32) * scale_of(sa_ref, sb_ref) * gain_ref[...]
    nb_ref[0] = normed.astype(BF16)
    gate = sigmoid(slope_ref[...] * normed + bias_ref[...])
    held[...] = (cot_ref[...].astype(F32) * gate).astype(BF16)
    for k, dest in enumerate(partners(n, 1)):
        outs[k][0] = held[pl.ds(pl.multiple_of(dest * size, size), size), :]


def gate_cotangent(n, tokens, cotangent, sa, sb, gain, slope, bias):
    rows, width = tokens.shape
    blocks = rows // B
    size = B // n
    tall = pl.BlockSpec((B, width), lambda a: (a, 0))
    row = pl.BlockSpec((8, B), lambda a: (0, a))
    vec = whole((1, width))
    result = pl.pallas_call(
        functools.partial(gate_kernel, n),
        grid=(blocks,),
        in_specs=[tall, tall, row, row, vec, vec, vec],
        out_specs=[pl.BlockSpec((1, B, width), lambda a: (a, 0, 0))]
        + [pl.BlockSpec((1, size, width), lambda a: (a, 0, 0))] * n,
        out_shape=[sds((blocks, B, width), BF16)] + [sds((blocks, size, width), BF16)] * n,
        scratch_shapes=[pltpu.VMEM((B, width), BF16)],
        compiler_params=params(),
        cost_estimate=cost(20 * rows * width, 8 * rows * width),
        name="gate_cotangent",
    )(tokens, cotangent, sa, sb, gain, slope, bias)
    return result[0], list(result[1:])


def twiddle_column(tw_ref, a):
    return column(jnp.broadcast_to(tw_ref[pl.ds(a, 1), :], (8, tw_ref.shape[1])))


def first_kernel(n, nb_ref, right_ref, tw_ref, *rest):
    first_ref, outs, held = rest[0], rest[1 : 1 + n], rest[1 + n]
    size = B // n
    first = jnp.dot(right_ref[...], nb_ref[0], preferred_element_type=F32)
    first_ref[0] = first
    held[...] = (first * twiddle_column(tw_ref, pl.program_id(0))).astype(BF16)
    for k, dest in enumerate(partners(n, 1)):
        outs[k][0] = held[pl.ds(pl.multiple_of(dest * size, size), size), :]


def first_factor(n, normed_b, right, twiddle):
    blocks, _, width = normed_b.shape
    size = B // n
    block = pl.BlockSpec((1, B, width), lambda a: (a, 0, 0))
    result = pl.pallas_call(
        functools.partial(first_kernel, n),
        grid=(blocks,),
        in_specs=[block, whole((B, B)), whole((blocks, B))],
        out_specs=[block] + [pl.BlockSpec((1, size, width), lambda a: (a, 0, 0))] * n,
        out_shape=[sds((blocks, B, width), F32)] + [sds((blocks, size, width), BF16)] * n,
        scratch_shapes=[pltpu.VMEM((B, width), BF16)],
        compiler_params=params(),
        cost_estimate=cost(2 * blocks * B * B * width, 8 * blocks * B * width),
        name="first_factor",
    )(normed_b, right, twiddle)
    return result[0], list(result[1:])


def group_of(n):
    return min(16, B // n)


def spread_matrix(rows, cols, group, offset, transposed):
    shape = (cols, rows) if transposed else (rows, cols)
    m = lax.broadcasted_iota(jnp.int32, shape, 1 if transposed else 0) + offset
    r = lax.broadcasted_iota(jnp.int32, shape, 0 if transposed else 1)
    inside = (m >= r * group) & (m < (r + 1) * group)
    return jnp.where(inside, 1.0, 0.0).astype(BF16)


def same_place(rows, cols, group, offset):
    m = lax.broadcasted_iota(jnp.int32, (rows, cols), 0) + offset
    q = lax.broadcasted_iota(jnp.int32, (rows, cols), 1)
    return lax.rem(m, group) == lax.rem(q, group)


def widen_kernel(group, left_ref, fore_ref, back_ref):
    step, total = fore_ref.shape
    outer = left_ref.shape[0]
    offset = pl.program_id(0) * step
    rows = spread_matrix(step, outer, group, offset, False)
    cols = spread_matrix(total, outer, group, 0, True)
    same = same_place(step, total, group, offset)
    left = left_ref[...]
    for source, out_ref in ((left, fore_ref), (left.astype(F32).T.astype(BF16), back_ref)):
        part = jnp.dot(rows, source, preferred_element_type=F32).astype(BF16)
        full = jnp.dot(part, cols, preferred_element_type=F32)
        out_ref[...] = jnp.where(same, full, 0.0).astype(BF16)


def widen(left, group):
    outer = left.shape[0]
    total = outer * group
    step = 256
    spec = pl.BlockSpec((step, total), lambda i: (i, 0))
    return pl.pallas_call(
        functools.partial(widen_kernel, group),
        grid=(total // step,),
        in_specs=[whole((outer, outer))],
        out_specs=[spec, spec],
        out_shape=[sds((total, total), BF16)] * 2,
        compiler_params=params(),
        cost_estimate=cost(4 * total * total * outer, 4 * total * total),
        name="widen",
    )(left)


def second_kernel(n, group, mat_ref, *rest):
    ins, outs, held, done = rest[:n], rest[n : 2 * n], rest[2 * n], rest[2 * n + 1]
    count, size, width = ins[0].shape
    sources, dests = partners(n, -1), partners(n, 1)
    span = count * group
    for g in range(size // group):
        part = pl.ds(g * group, group)
        for k in range(n):
            held[g, pl.ds(sources[k] * count, count)] = ins[k][:, part, :]
    for g in range(size // group):
        flat = held[g].reshape(-1, width)
        done[g] = jnp.dot(mat_ref[...], flat, preferred_element_type=F32).astype(BF16)
    for g in range(size // group):
        part = pl.ds(g * group, group)
        for k in range(n):
            place = pl.ds(pl.multiple_of(dests[k] * span, span), span)
            outs[k][:, part, :] = done[g, place, :].reshape(count, group, width)


def second_factor(n, matrix, blocks, name):
    count, size, width = blocks[0].shape
    group = group_of(n)
    total = matrix.shape[0]
    step = min(256, width)
    spec = pl.BlockSpec((count, size, step), lambda c: (0, 0, c))
    groups = size // group
    scratch = pltpu.VMEM((groups, n * count, group, step), BF16)
    return list(
        pl.pallas_call(
            functools.partial(second_kernel, n, group),
            grid=(width // step,),
            in_specs=[whole((total, total))] + [spec] * n,
            out_specs=[spec] * n,
            out_shape=[sds((count, size, width), BF16)] * n,
            scratch_shapes=[scratch, pltpu.VMEM((groups, total, step), BF16)],
            compiler_params=params(),
            cost_estimate=cost(2 * total * total * width * (size // group), 8 * n * count * size * width),
            name=name,
        )(matrix, *blocks)
    )


def left_kernel(n, group, *rest):
    cots, spreads, out_ref = rest[:n], rest[n : 2 * n], rest[2 * n]
    held_c, held_s, total_ref = rest[2 * n + 1 :]
    count, size, width = cots[0].shape
    sources = partners(n, -1)
    dims = (((1,), (1,)), ((), ()))

    @pl.when(pl.program_id(0) == 0)
    def _():
        total_ref[...] = jnp.zeros_like(total_ref)

    for g in range(size // group):
        part = pl.ds(g * group, group)
        for k in range(n):
            held_c[g, pl.ds(sources[k] * count, count)] = cots[k][:, part, :]
            held_s[g, pl.ds(sources[k] * count, count)] = spreads[k][:, part, :]
    for g in range(size // group):
        total_ref[...] += lax.dot_general(
            held_c[g].reshape(-1, width),
            held_s[g].reshape(-1, width),
            dims,
            preferred_element_type=F32,
        )

    @pl.when(pl.program_id(0) == pl.num_programs(0) - 1)
    def _():
        size_all = total_ref.shape[0]
        outer = size_all // group
        kept = jnp.where(same_place(size_all, size_all, group, 0), total_ref[...], 0.0)
        summed = kept.reshape(outer, group, size_all).sum(axis=1)
        gather = spread_matrix(size_all, outer, group, 0, False).astype(F32)
        out_ref[...] = jnp.dot(
            summed, gather, preferred_element_type=F32, precision=lax.Precision.HIGHEST
        )


def left_gradient(n, cots, spreads):
    count, size, width = cots[0].shape
    group = group_of(n)
    outer = n * count
    total = outer * group
    step = min(256, width)
    spec = pl.BlockSpec((count, size, step), lambda c: (0, 0, c))
    scratch = pltpu.VMEM((size // group, outer, group, step), BF16)
    return pl.pallas_call(
        functools.partial(left_kernel, n, group),
        grid=(width // step,),
        in_specs=[spec] * (2 * n),
        out_specs=whole((outer, outer)),
        out_shape=sds((outer, outer), F32),
        scratch_shapes=[scratch, scratch, pltpu.VMEM((total, total), F32)],
        compiler_params=params(),
        cost_estimate=cost(2 * total * total * width * (size // group), 8 * n * count * size * width),
        name="left_gradient",
    )(*cots, *spreads)


def back_kernel(n, first_ref, nb_ref, right_ref, tw_ref, *rest):
    ins, (twg_ref, rg_ref, mm_ref), (held, turned) = rest[:n], rest[n : n + 3], rest[n + 3 :]
    size = B // n
    a = pl.program_id(0)

    @pl.when(a == 0)
    def _():
        turned[...] = right_ref[...].astype(F32).T.astype(BF16)
        rg_ref[...] = jnp.zeros_like(rg_ref)

    for k, source in enumerate(partners(n, -1)):
        held[pl.ds(pl.multiple_of(source * size, size), size), :] = ins[k][0]
    grad = held[...].astype(F32)
    twg_ref[0] = row_sums(grad * first_ref[0])
    first_grad = (grad * twiddle_column(tw_ref, a)).astype(BF16)
    rg_ref[...] += lax.dot_general(
        first_grad, nb_ref[0], (((1,), (1,)), ((), ())), preferred_element_type=F32
    )
    mm_ref[0] = jnp.dot(turned[...], first_grad, preferred_element_type=F32)


def back_first(n, blocks, first_mix, normed_b, right, twiddle):
    count, _, width = normed_b.shape
    size = B // n
    block = pl.BlockSpec((1, B, width), lambda a: (a, 0, 0))
    return pl.pallas_call(
        functools.partial(back_kernel, n),
        grid=(count,),
        in_specs=[block, block, whole((B, B)), whole((count, B))]
        + [pl.BlockSpec((1, size, width), lambda a: (a, 0, 0))] * n,
        out_specs=[pl.BlockSpec((1, 8, B), lambda a: (a, 0, 0)), whole((B, B)), block],
        out_shape=[sds((count, 8, B), F32), sds((B, B), F32), sds((count, B, width), F32)],
        scratch_shapes=[pltpu.VMEM((B, width), BF16), pltpu.VMEM((B, B), BF16)],
        compiler_params=params(),
        cost_estimate=cost(4 * count * B * B * width, 12 * count * B * width),
        name="back_first",
    )(first_mix, normed_b, right, twiddle, *blocks)


def finish_kernel(n, tok_ref, cot_ref, sa_ref, sb_ref, gain_ref, slope_ref, bias_ref, mm_ref, *rest):
    ins, (mixed_ref, scaled_ref, inner_ref, sums_ref), held = rest[:n], rest[n : n + 4], rest[n + 4]
    size = B // n

    @pl.when(pl.program_id(0) == 0)
    def _():
        sums_ref[...] = jnp.zeros_like(sums_ref)

    for k, source in enumerate(partners(n, -1)):
        held[pl.ds(pl.multiple_of(source * size, size), size), :] = ins[k][0]
    second = held[...].astype(F32)
    wide = tok_ref[...].astype(F32)
    unit = wide * scale_of(sa_ref, sb_ref)
    normed = unit * gain_ref[...]
    gate = sigmoid(slope_ref[...] * normed + bias_ref[...])
    mixed_ref[...] = (gate * second).astype(BF16)
    gate_grad = cot_ref[...].astype(F32) * second * gate * (1.0 - gate)
    normed_grad = mm_ref[0] + gate_grad * slope_ref[...]
    scaled = normed_grad * gain_ref[...]
    scaled_ref[...] = scaled
    inner_ref[...] = row_sums(scaled * wide)
    sums_ref[0:1, :] += jnp.sum(normed_grad * unit, axis=0, keepdims=True)
    sums_ref[1:2, :] += jnp.sum(gate_grad * normed, axis=0, keepdims=True)
    sums_ref[2:3, :] += jnp.sum(gate_grad, axis=0, keepdims=True)


def finish(n, blocks, tokens, cotangent, sa, sb, gain, slope, bias, mm):
    rows, width = tokens.shape
    size = B // n
    tall = pl.BlockSpec((B, width), lambda a: (a, 0))
    row = pl.BlockSpec((8, B), lambda a: (0, a))
    vec = whole((1, width))
    return pl.pallas_call(
        functools.partial(finish_kernel, n),
        grid=(rows // B,),
        in_specs=[tall, tall, row, row, vec, vec, vec, pl.BlockSpec((1, B, width), lambda a: (a, 0, 0))]
        + [pl.BlockSpec((1, size, width), lambda a: (a, 0, 0))] * n,
        out_specs=[tall, tall, row, whole((8, width))],
        out_shape=[sds((rows, width), BF16), sds((rows, width), F32), sds((8, rows), F32), sds((8, width), F32)],
        scratch_shapes=[pltpu.VMEM((B, width), BF16)],
        compiler_params=params(),
        cost_estimate=cost(40 * rows * width, 16 * rows * width),
        name="finish",
    )(tokens, cotangent, sa, sb, gain, slope, bias, mm, *blocks)


def token_kernel(tok_ref, scaled_ref, sa_ref, sb_ref, ia_ref, ib_ref, out_ref):
    scale = lax.rsqrt((sa_ref[...] + sb_ref[...]) / D + EPS)
    inner = (ia_ref[...] + ib_ref[...]) * (scale * scale * scale) / D
    out_ref[...] = (
        column(scale) * scaled_ref[...] - tok_ref[...].astype(F32) * column(inner)
    ).astype(BF16)


def token_gradient(tokens, scaled, sa, sb, ia, ib):
    rows, width = tokens.shape
    tall = pl.BlockSpec((B, width), lambda a: (a, 0))
    row = pl.BlockSpec((8, B), lambda a: (0, a))
    return pl.pallas_call(
        token_kernel,
        grid=(rows // B,),
        in_specs=[tall, tall, row, row, row, row],
        out_specs=tall,
        out_shape=sds((rows, width), BF16),
        compiler_params=params(),
        cost_estimate=cost(5 * rows * width, 8 * rows * width),
        name="token_gradient",
    )(tokens, scaled, sa, sb, ia, ib)


def on_device(
    tokens, cotangent, norm_gain, gate_slope, gate_bias, right_factor, left_factor, twiddle
):
    n = lax.axis_size("seq")
    rows, width = tokens.shape
    gain, slope, bias = (v.reshape(1, width) for v in (norm_gain, gate_slope, gate_bias))
    sa, sb = chan_terms(squares(tokens))
    normed_b, cot_blocks = gate_cotangent(n, tokens, cotangent, sa, sb, gain, slope, bias)
    cot_cols = exchange(cot_blocks)
    right = chan_gather(right_factor)
    first_mix, spread_blocks = first_factor(n, normed_b, right, twiddle)
    spread_cols = exchange(spread_blocks)
    fore, back = widen(chan_gather(left_factor), group_of(n))

    cot_cols, spread_cols = after_part(cot_cols, spread_cols)
    grad_back = exchange(second_factor(n, back, cot_cols, "spread_grad"))
    spread_cols, grad_back = after_part(spread_cols, grad_back)
    mix_back = exchange(second_factor(n, fore, spread_cols, "second_mix"))
    left_part = left_gradient(n, cot_cols, spread_cols)
    grad_back, mix_back = after_part(grad_back, mix_back)
    twiddle_rows, right_part, mm = back_first(n, grad_back, first_mix, normed_b, right, twiddle)
    ta, tb = chan_terms(twiddle_rows)
    twiddle_grad = ta[:, 0] + tb[:, 0]
    right_part = chan_scatter(right_part)
    left_part = chan_scatter(left_part)

    mixed, scaled, inner, sums = finish(
        n, mix_back, tokens, cotangent, sa, sb, gain, slope, bias, mm
    )
    ia, ib = chan_terms(inner)
    token_grad = token_gradient(tokens, scaled, sa, sb, ia, ib)

    right_flat = right_part.reshape(n, -1)
    left_flat = left_part.reshape(n, -1)
    small = jnp.broadcast_to(sums[:3].reshape(1, -1), (n, 3 * width))
    sizes = [right_flat.shape[1], left_flat.shape[1]]
    parts = lax.all_to_all(
        jnp.concatenate([right_flat, left_flat, small], axis=1), "seq", 0, 0
    )
    total = jnp.sum(parts, axis=0)
    right_out = total[: sizes[0]].reshape(B // n, -1)
    left_out = total[sizes[0] : sizes[0] + sizes[1]].reshape(left_part.shape[0] // n, -1)
    vectors = total[sizes[0] + sizes[1] :].reshape(3, width)
    return (
        mixed,
        token_grad,
        right_out,
        left_out,
        twiddle_grad,
        vectors[0],
        vectors[1],
        vectors[2],
    )


def solution(mesh):
    return jax.shard_map(
        on_device,
        mesh=mesh,
        in_specs=(
            P("seq", "chan"),
            P("seq", "chan"),
            P("chan"),
            P("chan"),
            P("chan"),
            P("chan", None),
            P("chan", None),
            P("seq", None),
        ),
        out_specs=(
            P("seq", "chan"),
            P("seq", "chan"),
            P("seq", "chan"),
            P("seq", "chan"),
            P("seq", None),
            P("chan"),
            P("chan"),
            P("chan"),
        ),
        check_vma=False,
    )
```

```python
import functools

import jax
import jax.numpy as jnp
from jax import lax
from jax.experimental import pallas as pl
from jax.experimental.pallas import tpu as pltpu
from jax.sharding import PartitionSpec as P

D = 1024
B = 512
EPS = 1e-05
LAG = 8
LAST = 10
SHARE = 1000

F32 = jnp.float32
BF16 = jnp.bfloat16


def sds(shape, dtype):
    return jax.ShapeDtypeStruct(shape, dtype)


def cost(flops, nbytes):
    return pl.CostEstimate(flops=int(flops) // SHARE, bytes_accessed=int(nbytes) // SHARE, transcendentals=0)


def params(mib=20):
    return pltpu.CompilerParams(vmem_limit_bytes=mib * 1024 * 1024)


def whole(shape):
    zeros = (0,) * len(shape)
    return pl.BlockSpec(shape, lambda *_: zeros)


HBM = pl.BlockSpec(memory_space=pltpu.HBM)
VMEM = pl.BlockSpec(memory_space=pltpu.VMEM)


def partners(n, sign):
    me = lax.axis_index("seq")
    hi, lo = me // 4, me % 4
    high = n // 4
    lo_of = [lo, lo + 1 - 2 * (lo % 2), (lo + 2) % 4, 3 - lo]
    return [
        ((hi + (sign * (k // 4)) % high) % high) * 4 + lo_of[k % 4]
        for k in range(n)
    ]


def pairs(n, k):
    high = n // 4
    return [
        (i, ((i // 4 + k // 4) % high) * 4 + ((i % 4) ^ (k % 4)))
        for i in range(n)
    ]


def send_order(n):
    high = n // 4
    far_first = sorted(range(1, high), key=lambda d: (abs(d - high / 2), d))
    order = []
    for dl in range(4):
        order += [4 * dh + dl for dh in far_first]
        if dl < 3:
            order.append(dl + 1)
    return order


def exchange(blocks):
    n = len(blocks)
    out = list(blocks)
    for k in send_order(n):
        out[k] = lax.ppermute(blocks[k], "seq", pairs(n, k))
    return out


def in_hbm(blocks):
    return [pltpu.with_memory_space_constraint(x, pltpu.HBM) for x in blocks]


def after_part(values, started, count=LAG):
    keys = send_order(len(started))[:count]
    values, held = lax.optimization_barrier((values, [started[k] for k in keys]))
    started = list(started)
    for k, v in zip(keys, held):
        started[k] = v
    return values, started


def chan_terms(x):
    nc = lax.axis_size("chan")
    if nc == 2:
        return x, lax.ppermute(x, "chan", [(0, 1), (1, 0)])
    return lax.psum(x, "chan"), jnp.zeros_like(x)


def chan_gather(x):
    nc = lax.axis_size("chan")
    if nc != 2:
        return lax.all_gather(x, "chan", axis=0, tiled=True)
    other = lax.ppermute(x, "chan", [(0, 1), (1, 0)])
    first = lax.axis_index("chan") == 0
    return jnp.concatenate(
        [jnp.where(first, x, other), jnp.where(first, other, x)], axis=0
    )


def chan_halves(x):
    half = x.shape[1] // 2
    first = lax.axis_index("chan") == 0
    low, high = x[:, :half], x[:, half:]
    return jnp.where(first, low, high), jnp.where(first, high, low)


def chan_joined(keep, give):
    if lax.axis_size("chan") == 2:
        return keep, lax.ppermute(give, "chan", [(0, 1), (1, 0)])
    out = lax.psum_scatter(give, "chan", scatter_dimension=1, tiled=True)
    return out, jnp.zeros_like(out)


def flipped(x, bit):
    n = lax.axis_size("seq")
    return lax.ppermute(x, "seq", [(i, i ^ bit) for i in range(n)])


def bits(n):
    return [1 << i for i in range(n.bit_length() - 1)]


def write_split(bit, blocks, keep_ref, message):
    mine = (lax.axis_index("seq") // bit) % 2
    size = keep_ref.shape[1]
    for q in range(keep_ref.shape[0]):
        keep_ref[q] = blocks(2 * q + mine)
        message[q * size : (q + 1) * size, :] = blocks(2 * q + 1 - mine)


def join_kernel(bit, ra_ref, rb_ref, la_ref, lb_ref, sums_ref, keep_ref, message, held):
    n, size, width = held.shape
    rows = size - 8
    count = la_ref.shape[0] // n
    thin = la_ref.shape[1]
    held[:, :rows, :] = (ra_ref[...] + rb_ref[...]).reshape(n, rows, width)
    held[:, rows:, :] = jnp.zeros((n, 8, width), F32)
    left = la_ref[...] + lb_ref[...]
    for q in range(n):
        held[q, rows : rows + count, :thin] = left[q * count : (q + 1) * count, :]
    write_split(bit, lambda q: held[q], keep_ref, message)
    message[n // 2 * size :, :] = sums_ref[...]


def join(bit, n, ra, rb, la, lb, sums):
    rows, width = ra.shape
    size = rows // n + 8
    return pl.pallas_call(
        functools.partial(join_kernel, bit),
        in_specs=[VMEM] * 5,
        out_specs=[VMEM] * 2,
        out_shape=[
            sds((n // 2, size, width), F32),
            sds((n // 2 * size + sums.shape[0], width), F32),
        ],
        scratch_shapes=[pltpu.VMEM((n, size, width), F32)],
        compiler_params=params(8),
        cost_estimate=cost(rows * width, 8 * rows * width),
        name="join",
    )(ra, rb, la, lb, sums)


def fold_kernel(bit, keep_ref, small_ref, came, next_keep, next_small, message):
    parts, size, _ = keep_ref.shape
    write_split(
        bit,
        lambda q: keep_ref[q] + came[pl.ds(pl.multiple_of(q * size, 8), size), :],
        next_keep,
        message,
    )
    small = small_ref[...] + came[parts * size :, :]
    next_small[...] = small
    message[parts // 2 * size :, :] = small


def fold(bit, keep, small, came):
    parts, size, width = keep.shape
    tail = small.shape[0]
    shapes = [
        sds((parts // 2, size, width), F32),
        sds((tail, width), F32),
        sds((parts // 2 * size + tail, width), F32),
    ]
    return pl.pallas_call(
        functools.partial(fold_kernel, bit),
        in_specs=[VMEM] * 3,
        out_specs=[VMEM] * 3,
        out_shape=shapes,
        compiler_params=params(8),
        cost_estimate=cost(parts * size * width, 8 * parts * size * width),
        name="fold",
    )(keep, small, came)


def close_kernel(keep_ref, small_ref, came, ta_ref, tb_ref, right_ref, left_ref, twiddle_ref, *vectors):
    _, size, width = keep_ref.shape
    rows, count, thin = size - 8, *left_ref.shape
    right_ref[...] = keep_ref[0, :rows, :] + came[:rows, :]
    left_ref[...] = keep_ref[0, rows : rows + count, :thin] + came[rows : rows + count, :thin]
    small = small_ref[...] + came[size:, :]
    lines = vectors[0].shape[1] // width
    for i, out_ref in enumerate(vectors):
        for j in range(lines):
            at = i * lines + j
            out_ref[:, j * width : (j + 1) * width] = small[at : at + 1, :]
    for a in range(twiddle_ref.shape[0]):
        twiddle_ref[a : a + 1, :] = ta_ref[a, :1, :] + tb_ref[a, :1, :]


def close(keep, small, came, ta, tb, count, thin, chans):
    _, size, width = keep.shape
    return pl.pallas_call(
        close_kernel,
        in_specs=[VMEM] * 5,
        out_shape=[
            sds((size - 8, width), F32),
            sds((count, thin), F32),
            sds((ta.shape[0], ta.shape[2]), F32),
        ]
        + [sds((1, chans), F32)] * 3,
        compiler_params=params(8),
        cost_estimate=cost(size * width, 8 * size * width),
        name="close",
    )(keep, small, came, ta, tb)


def row_sums(x):
    high = x.astype(BF16)
    low = (x - high.astype(F32)).astype(BF16)
    ones = jnp.ones((x.shape[1], 128), BF16)
    sums = jnp.dot(high, ones, preferred_element_type=F32) + jnp.dot(
        low, ones, preferred_element_type=F32
    )
    return sums.T[:8, :]


def column(rows):
    return rows.T[:, :1]


def scale_of(sa_ref, sb_ref):
    return column(lax.rsqrt((sa_ref[...] + sb_ref[...]) / D + EPS))


def sigmoid(x):
    return 0.5 * jnp.tanh(0.5 * x) + 0.5


def squares_kernel(tok_ref, out_ref):
    x = tok_ref[...].astype(F32)
    out_ref[...] = row_sums(x * x)


def squares(tokens):
    rows, width = tokens.shape
    return pl.pallas_call(
        squares_kernel,
        grid=(rows // B,),
        in_specs=[pl.BlockSpec((B, width), lambda a: (a, 0))],
        out_specs=pl.BlockSpec((8, B), lambda a: (0, a)),
        out_shape=sds((8, rows), F32),
        compiler_params=params(),
        cost_estimate=cost(8 * rows * width, 2 * rows * width),
        name="squares",
    )(tokens)


def gate_kernel(n, tok_ref, cot_ref, sa_ref, sb_ref, gain_ref, slope_ref, bias_ref, *rest):
    nb_ref, outs, held = rest[0], rest[1 : 1 + n], rest[1 + n]
    size = B // n
    normed = tok_ref[...].astype(F32) * scale_of(sa_ref, sb_ref) * gain_ref[...]
    nb_ref[0] = normed.astype(BF16)
    gate = sigmoid(slope_ref[...] * normed + bias_ref[...])
    held[...] = (cot_ref[...].astype(F32) * gate).astype(BF16)
    for k, dest in enumerate(partners(n, 1)):
        outs[k][0] = held[pl.ds(pl.multiple_of(dest * size, size), size), :]


def gate_cotangent(n, tokens, cotangent, sa, sb, gain, slope, bias):
    rows, width = tokens.shape
    blocks = rows // B
    size = B // n
    tall = pl.BlockSpec((B, width), lambda a: (a, 0))
    row = pl.BlockSpec((8, B), lambda a: (0, a))
    vec = whole((1, width))
    result = pl.pallas_call(
        functools.partial(gate_kernel, n),
        grid=(blocks,),
        in_specs=[tall, tall, row, row, vec, vec, vec],
        out_specs=[pl.BlockSpec((1, B, width), lambda a: (a, 0, 0))]
        + [pl.BlockSpec((1, size, width), lambda a: (a, 0, 0))] * n,
        out_shape=[sds((blocks, B, width), BF16)] + [sds((blocks, size, width), BF16)] * n,
        scratch_shapes=[pltpu.VMEM((B, width), BF16)],
        compiler_params=params(),
        cost_estimate=cost(20 * rows * width, 8 * rows * width),
        name="gate_cotangent",
    )(tokens, cotangent, sa, sb, gain, slope, bias)
    return result[0], list(result[1:])


def twiddle_column(tw_ref, a):
    return column(jnp.broadcast_to(tw_ref[pl.ds(a, 1), :], (8, tw_ref.shape[1])))


def first_kernel(n, nb_ref, right_ref, tw_ref, *rest):
    first_ref, outs, held = rest[0], rest[1 : 1 + n], rest[1 + n]
    size = B // n
    first = jnp.dot(right_ref[...], nb_ref[0], preferred_element_type=F32)
    first_ref[0] = first
    held[...] = (first * twiddle_column(tw_ref, pl.program_id(0))).astype(BF16)
    for k, dest in enumerate(partners(n, 1)):
        outs[k][0] = held[pl.ds(pl.multiple_of(dest * size, size), size), :]


def first_factor(n, normed_b, right, twiddle):
    blocks, _, width = normed_b.shape
    size = B // n
    block = pl.BlockSpec((1, B, width), lambda a: (a, 0, 0))
    result = pl.pallas_call(
        functools.partial(first_kernel, n),
        grid=(blocks,),
        in_specs=[block, whole((B, B)), whole((blocks, B))],
        out_specs=[block] + [pl.BlockSpec((1, size, width), lambda a: (a, 0, 0))] * n,
        out_shape=[sds((blocks, B, width), F32)] + [sds((blocks, size, width), BF16)] * n,
        scratch_shapes=[pltpu.VMEM((B, width), BF16)],
        compiler_params=params(),
        cost_estimate=cost(2 * blocks * B * B * width, 8 * blocks * B * width),
        name="first_factor",
    )(normed_b, right, twiddle)
    return result[0], list(result[1:])


def group_of(n):
    return min(16, B // n)


def spread_matrix(rows, cols, group, offset, transposed):
    shape = (cols, rows) if transposed else (rows, cols)
    m = lax.broadcasted_iota(jnp.int32, shape, 1 if transposed else 0) + offset
    r = lax.broadcasted_iota(jnp.int32, shape, 0 if transposed else 1)
    inside = (m >= r * group) & (m < (r + 1) * group)
    return jnp.where(inside, 1.0, 0.0).astype(BF16)


def same_place(rows, cols, group, offset):
    m = lax.broadcasted_iota(jnp.int32, (rows, cols), 0) + offset
    q = lax.broadcasted_iota(jnp.int32, (rows, cols), 1)
    return lax.rem(m, group) == lax.rem(q, group)


def widen_kernel(group, left_ref, fore_ref, back_ref):
    step, total = fore_ref.shape
    outer = left_ref.shape[0]
    offset = pl.program_id(0) * step
    rows = spread_matrix(step, outer, group, offset, False)
    cols = spread_matrix(total, outer, group, 0, True)
    same = same_place(step, total, group, offset)
    left = left_ref[...]
    for source, out_ref in ((left, fore_ref), (left.astype(F32).T.astype(BF16), back_ref)):
        part = jnp.dot(rows, source, preferred_element_type=F32).astype(BF16)
        full = jnp.dot(part, cols, preferred_element_type=F32)
        out_ref[...] = jnp.where(same, full, 0.0).astype(BF16)


def widen(left, group):
    outer = left.shape[0]
    total = outer * group
    step = 256
    spec = pl.BlockSpec((step, total), lambda i: (i, 0))
    return pl.pallas_call(
        functools.partial(widen_kernel, group),
        grid=(total // step,),
        in_specs=[whole((outer, outer))],
        out_specs=[spec, spec],
        out_shape=[sds((total, total), BF16)] * 2,
        compiler_params=params(),
        cost_estimate=cost(4 * total * total * outer, 4 * total * total),
        name="widen",
    )(left)


def fetch(pairs_of_refs, sems):
    copies = [
        pltpu.make_async_copy(source, target, sems.at[i])
        for i, (source, target) in enumerate(pairs_of_refs)
    ]
    for copy in copies:
        copy.start()
    return copies


def group_copies(ins, held, group):
    n = len(ins)
    count, size, _ = ins[0].shape
    sources = partners(n, -1)
    return [
        (
            ins[k].at[:, pl.ds(g * group, group), :],
            held.at[g, pl.ds(sources[k] * count, count), :, :],
        )
        for g in range(size // group)
        for k in range(n)
    ]


def second_kernel(n, group, mat_ref, *rest):
    ins, outs, held, done, sems = rest[:n], rest[n : 2 * n], *rest[2 * n :]
    count, size, width = outs[0].shape
    groups = size // group
    dests = partners(n, 1)
    copies = fetch(group_copies(ins, held, group), sems)
    span = count * group
    step = min(256, width)
    for g in range(groups):
        for copy in copies[g * n : (g + 1) * n]:
            copy.wait()
        for c in range(width // step):
            part = slice(c * step, (c + 1) * step)
            flat = held[g, :, :, part].reshape(-1, step)
            done[g, :, part] = jnp.dot(
                mat_ref[...], flat, preferred_element_type=F32
            ).astype(BF16)
        for k in range(n):
            place = pl.ds(pl.multiple_of(dests[k] * span, span), span)
            outs[k][:, pl.ds(g * group, group), :] = done[g, place, :].reshape(count, group, width)


def second_factor(n, matrix, blocks, name):
    count, size, width = blocks[0].shape
    group = group_of(n)
    groups = size // group
    total = matrix.shape[0]
    return list(
        pl.pallas_call(
            functools.partial(second_kernel, n, group),
            in_specs=[VMEM] + [HBM] * n,
            out_shape=[sds((count, size, width), BF16)] * n,
            scratch_shapes=[
                pltpu.VMEM((groups, n * count, group, width), BF16),
                pltpu.VMEM((groups, total, width), BF16),
                pltpu.SemaphoreType.DMA((groups * n,)),
            ],
            compiler_params=params(),
            cost_estimate=cost(2 * total * total * width * groups, 8 * n * count * size * width),
            name=name,
        )(matrix, *in_hbm(blocks))
    )


def halves(rows, columns):
    nc = lax.axis_size("chan")
    if nc == 2:
        return [sds((rows, columns // 2), F32)] * 2
    return [sds((8, 128), F32), sds((rows, columns), F32)]


def store_halves(full, keep_ref, give_ref):
    if lax.axis_size("chan") == 2:
        keep_ref[...], give_ref[...] = chan_halves(full)
    else:
        keep_ref[...] = jnp.zeros_like(keep_ref)
        give_ref[...] = full


def left_kernel(n, group, *rest):
    cots, spreads, keep_ref, give_ref = rest[:n], rest[n : 2 * n], *rest[2 * n : 2 * n + 2]
    held_c, held_s, summed, sems = rest[2 * n + 2 :]
    groups, outer, _, width = held_c.shape
    dims = (((1,), (1,)), ((), ()))
    total = outer * group
    step = min(256, total)
    copies = fetch(group_copies(cots, held_c, group) + group_copies(spreads, held_s, group), sems)
    for copy in copies:
        copy.wait()
    for r in range(total // step):
        product = sum(
            lax.dot_general(
                held_c[g, r * step // group : (r + 1) * step // group].reshape(step, width),
                held_s[g].reshape(total, width),
                dims,
                preferred_element_type=F32,
            )
            for g in range(groups)
        )
        kept = jnp.where(same_place(step, total, group, 0), product, 0.0)
        lines = step // group
        summed[r * lines : (r + 1) * lines, :] = kept.reshape(lines, group, total).sum(axis=1)
    gather = spread_matrix(total, outer, group, 0, False).astype(F32)
    full = jnp.dot(
        summed[...], gather, preferred_element_type=F32, precision=lax.Precision.HIGHEST
    )
    store_halves(full, keep_ref, give_ref)


def left_gradient(n, cots, spreads):
    count, size, width = cots[0].shape
    group = group_of(n)
    outer = n * count
    total = outer * group
    groups = size // group
    scratch = pltpu.VMEM((groups, outer, group, width), BF16)
    return pl.pallas_call(
        functools.partial(left_kernel, n, group),
        in_specs=[HBM] * (2 * n),
        out_shape=halves(outer, outer),
        scratch_shapes=[
            scratch,
            scratch,
            pltpu.VMEM((outer, total), F32),
            pltpu.SemaphoreType.DMA((2 * groups * n,)),
        ],
        compiler_params=params(),
        cost_estimate=cost(2 * total * total * width * (size // group), 8 * n * count * size * width),
        name="left_gradient",
    )(*in_hbm(cots), *in_hbm(spreads))


def row_copies(ins, held):
    n = len(ins)
    size = ins[0].shape[1]
    return [
        (ins[k], held.at[:, pl.ds(pl.multiple_of(source * size, size), size), :])
        for k, source in enumerate(partners(n, -1))
    ]


def back_kernel(n, first_ref, nb_ref, right_ref, tw_ref, *rest):
    ins, (twg_ref, mm_ref, keep_ref, give_ref), (held, sems) = rest[:n], rest[n : n + 4], rest[n + 4 :]
    copies = fetch(row_copies(ins, held), sems)
    turned = right_ref[...].astype(F32).T.astype(BF16)
    for copy in copies:
        copy.wait()
    total = None
    for a in range(nb_ref.shape[0]):
        grad = held[a].astype(F32)
        twg_ref[a] = row_sums(grad * first_ref[a])
        first_grad = (grad * twiddle_column(tw_ref, a)).astype(BF16)
        mm_ref[a] = jnp.dot(turned, first_grad, preferred_element_type=F32)
        part = lax.dot_general(
            first_grad, nb_ref[a], (((1,), (1,)), ((), ())), preferred_element_type=F32
        )
        total = part if a == 0 else total + part
    store_halves(total, keep_ref, give_ref)


def back_first(n, blocks, first_mix, normed_b, right, twiddle):
    count, _, width = normed_b.shape
    return pl.pallas_call(
        functools.partial(back_kernel, n),
        in_specs=[VMEM] * 4 + [HBM] * n,
        out_specs=[VMEM] * 4,
        out_shape=[sds((count, 8, B), F32), sds((count, B, width), F32)] + halves(B, B),
        scratch_shapes=[pltpu.VMEM((count, B, width), BF16), pltpu.SemaphoreType.DMA((n,))],
        compiler_params=params(),
        cost_estimate=cost(4 * count * B * B * width, 12 * count * B * width),
        name="back_first",
    )(first_mix, normed_b, right, twiddle, *in_hbm(blocks))


def finish_kernel(n, tok_ref, cot_ref, sa_ref, sb_ref, gain_ref, slope_ref, bias_ref, mm_ref, *rest):
    ins, (mixed_ref, scaled_ref, inner_ref, sums_ref), (held, sems) = (
        rest[:n],
        rest[n : n + 4],
        rest[n + 4 :],
    )
    copies = fetch(row_copies(ins, held), sems)
    for copy in copies:
        copy.wait()
    scale = lax.rsqrt((sa_ref[...] + sb_ref[...]) / D + EPS)
    gains, slopes, biases = [], [], []
    for a in range(mm_ref.shape[0]):
        rows = slice(a * B, (a + 1) * B)
        second = held[a].astype(F32)
        wide = tok_ref[rows, :].astype(F32)
        unit = wide * column(scale[:, rows])
        normed = unit * gain_ref[...]
        gate = sigmoid(slope_ref[...] * normed + bias_ref[...])
        mixed_ref[rows, :] = (gate * second).astype(BF16)
        gate_grad = cot_ref[rows, :].astype(F32) * second * gate * (1.0 - gate)
        normed_grad = mm_ref[a] + gate_grad * slope_ref[...]
        scaled = normed_grad * gain_ref[...]
        scaled_ref[rows, :] = scaled
        inner_ref[:, rows] = row_sums(scaled * wide)
        gains.append(jnp.sum(normed_grad * unit, axis=0, keepdims=True))
        slopes.append(jnp.sum(gate_grad * normed, axis=0, keepdims=True))
        biases.append(jnp.sum(gate_grad, axis=0, keepdims=True))
    for i, terms in enumerate((gains, slopes, biases)):
        line = sum(terms)
        part = sums_ref.shape[1]
        lines = line.shape[1] // part
        for j in range(lines):
            at = i * lines + j
            sums_ref[at : at + 1, :] = line[:, j * part : (j + 1) * part]
    for at in range(3 * lines, sums_ref.shape[0]):
        sums_ref[at : at + 1, :] = jnp.zeros((1, part), F32)


def finish(n, blocks, tokens, cotangent, sa, sb, gain, slope, bias, mm, part):
    rows, width = tokens.shape
    return pl.pallas_call(
        functools.partial(finish_kernel, n),
        in_specs=[VMEM] * 8 + [HBM] * n,
        out_specs=[VMEM] * 4,
        out_shape=[sds((rows, width), BF16), sds((rows, width), F32), sds((8, rows), F32), sds((8, part), F32)],
        scratch_shapes=[pltpu.VMEM((rows // B, B, width), BF16), pltpu.SemaphoreType.DMA((n,))],
        compiler_params=params(),
        cost_estimate=cost(40 * rows * width, 16 * rows * width),
        name="finish",
    )(tokens, cotangent, sa, sb, gain, slope, bias, mm, *in_hbm(blocks))


def token_kernel(tok_ref, scaled_ref, sa_ref, sb_ref, ia_ref, ib_ref, out_ref):
    scale = lax.rsqrt((sa_ref[...] + sb_ref[...]) / D + EPS)
    inner = (ia_ref[...] + ib_ref[...]) * (scale * scale * scale) / D
    out_ref[...] = (
        column(scale) * scaled_ref[...] - tok_ref[...].astype(F32) * column(inner)
    ).astype(BF16)


def token_gradient(tokens, scaled, sa, sb, ia, ib):
    rows, width = tokens.shape
    tall = pl.BlockSpec((B, width), lambda a: (a, 0))
    row = pl.BlockSpec((8, B), lambda a: (0, a))
    return pl.pallas_call(
        token_kernel,
        grid=(rows // B,),
        in_specs=[tall, tall, row, row, row, row],
        out_specs=tall,
        out_shape=sds((rows, width), BF16),
        compiler_params=params(),
        cost_estimate=cost(5 * rows * width, 8 * rows * width),
        name="token_gradient",
    )(tokens, scaled, sa, sb, ia, ib)


def on_device(
    tokens, cotangent, norm_gain, gate_slope, gate_bias, right_factor, left_factor, twiddle
):
    n = lax.axis_size("seq")
    rows, width = tokens.shape
    gain, slope, bias = (v.reshape(1, width) for v in (norm_gain, gate_slope, gate_bias))
    sa, sb = chan_terms(squares(tokens))
    normed_b, cot_blocks = gate_cotangent(n, tokens, cotangent, sa, sb, gain, slope, bias)
    cot_cols = exchange(cot_blocks)
    right = chan_gather(right_factor)
    first_mix, spread_blocks = first_factor(n, normed_b, right, twiddle)
    spread_cols = exchange(spread_blocks)
    fore, back = widen(chan_gather(left_factor), group_of(n))

    cot_cols, spread_cols = after_part(cot_cols, spread_cols)
    grad_back = exchange(second_factor(n, back, cot_cols, "spread_grad"))
    spread_cols, grad_back = after_part(spread_cols, grad_back)
    mix_blocks = second_factor(n, fore, spread_cols, "second_mix")
    left_keep, left_give = left_gradient(n, cot_cols, spread_cols)
    la, lb = chan_joined(left_keep, left_give)
    left_give, mix_blocks = lax.optimization_barrier((left_give, mix_blocks))
    mix_back = exchange(mix_blocks)
    grad_back, mix_back = after_part(grad_back, mix_back, LAST)
    twiddle_rows, mm, right_keep, right_give = back_first(
        n, grad_back, first_mix, normed_b, right, twiddle
    )
    part = B // lax.axis_size("chan")
    mixed, scaled, inner, sums = finish(
        n, mix_back, tokens, cotangent, sa, sb, gain, slope, bias, mm, part
    )
    right_give, twiddle_rows, sums = lax.optimization_barrier((right_give, twiddle_rows, sums))
    ra, rb = chan_joined(right_keep, right_give)
    ia, ib = chan_terms(inner)
    token_grad = token_gradient(tokens, scaled, sa, sb, ia, ib)
    steps = bits(n)
    keep, message = join(steps[0], n, ra, rb, la, lb, sums)
    came = flipped(message, steps[0])
    for bit in steps[1:]:
        keep, sums, message = fold(bit, keep, sums, came)
        came = flipped(message, bit)
    ta, tb = chan_terms(twiddle_rows)
    right_out, left_out, twiddle_grad, *vectors = close(
        keep, sums, came, ta, tb, la.shape[0] // n, la.shape[1], width
    )
    return (mixed, token_grad, right_out, left_out, twiddle_grad, *(v.reshape(-1) for v in vectors))


def solution(mesh):
    return jax.shard_map(
        on_device,
        mesh=mesh,
        in_specs=(
            P("seq", "chan"),
            P("seq", "chan"),
            P("chan"),
            P("chan"),
            P("chan"),
            P("chan", None),
            P("chan", None),
            P("seq", None),
        ),
        out_specs=(
            P("seq", "chan"),
            P("seq", "chan"),
            P("seq", "chan"),
            P("seq", "chan"),
            P("seq", None),
            P("chan"),
            P("chan"),
            P("chan"),
        ),
        check_vma=False,
    )
```

```python
import functools

import jax
import jax.numpy as jnp
from jax import lax
from jax.experimental import pallas as pl
from jax.experimental.pallas import tpu as pltpu
from jax.sharding import PartitionSpec as P

D = 1024
B = 512
EPS = 1e-05
LAG = 8
LAST = 6
SHARE = 1000

F32 = jnp.float32
BF16 = jnp.bfloat16


def sds(shape, dtype):
    return jax.ShapeDtypeStruct(shape, dtype)


def cost(flops, nbytes):
    return pl.CostEstimate(flops=int(flops) // SHARE, bytes_accessed=int(nbytes) // SHARE, transcendentals=0)


def params(mib=20):
    return pltpu.CompilerParams(vmem_limit_bytes=mib * 1024 * 1024)


def whole(shape):
    zeros = (0,) * len(shape)
    return pl.BlockSpec(shape, lambda *_: zeros)


HBM = pl.BlockSpec(memory_space=pltpu.HBM)
VMEM = pl.BlockSpec(memory_space=pltpu.VMEM)


def partners(n, sign):
    me = lax.axis_index("seq")
    hi, lo = me // 4, me % 4
    high = n // 4
    lo_of = [lo, lo + 1 - 2 * (lo % 2), (lo + 2) % 4, 3 - lo]
    return [
        ((hi + (sign * (k // 4)) % high) % high) * 4 + lo_of[k % 4]
        for k in range(n)
    ]


def pairs(n, k):
    high = n // 4
    return [
        (i, ((i // 4 + k // 4) % high) * 4 + ((i % 4) ^ (k % 4)))
        for i in range(n)
    ]


def send_order(n):
    if n == 16:
        return [1, 8, 4, 12, 2, 9, 5, 13, 3, 10, 6, 14, 11, 7, 15]
    high = n // 4
    far_first = sorted(range(1, high), key=lambda d: (abs(d - high / 2), d))
    order = []
    for dl in range(4):
        order += [4 * dh + dl for dh in far_first]
        if dl < 3:
            order.append(dl + 1)
    return order


def exchange(blocks):
    n = len(blocks)
    out = list(blocks)
    for k in send_order(n):
        out[k] = lax.ppermute(blocks[k], "seq", pairs(n, k))
    return out


def in_hbm(blocks):
    return [pltpu.with_memory_space_constraint(x, pltpu.HBM) for x in blocks]


def after_part(values, started, count=LAG):
    keys = send_order(len(started))[:count]
    values, held = lax.optimization_barrier((values, [started[k] for k in keys]))
    started = list(started)
    for k, v in zip(keys, held):
        started[k] = v
    return values, started


def chan_terms(x):
    nc = lax.axis_size("chan")
    if nc == 2:
        return x, lax.ppermute(x, "chan", [(0, 1), (1, 0)])
    return lax.psum(x, "chan"), jnp.zeros_like(x)


def chan_gather(x):
    nc = lax.axis_size("chan")
    if nc != 2:
        return lax.all_gather(x, "chan", axis=0, tiled=True)
    other = lax.ppermute(x, "chan", [(0, 1), (1, 0)])
    first = lax.axis_index("chan") == 0
    return jnp.concatenate(
        [jnp.where(first, x, other), jnp.where(first, other, x)], axis=0
    )


def chan_halves(x):
    half = x.shape[1] // 2
    first = lax.axis_index("chan") == 0
    low, high = x[:, :half], x[:, half:]
    return jnp.where(first, low, high), jnp.where(first, high, low)


def chan_joined(keep, give):
    if lax.axis_size("chan") == 2:
        return keep, lax.ppermute(give, "chan", [(0, 1), (1, 0)])
    out = lax.psum_scatter(give, "chan", scatter_dimension=1, tiled=True)
    return out, jnp.zeros_like(out)


def flipped(x, bit):
    n = lax.axis_size("seq")
    return lax.ppermute(x, "seq", [(i, i ^ bit) for i in range(n)])


def bits(n):
    return [1 << i for i in range(n.bit_length() - 1)]


def write_split(bit, blocks, keep_ref, message):
    mine = (lax.axis_index("seq") // bit) % 2
    size = keep_ref.shape[1]
    for q in range(keep_ref.shape[0]):
        keep_ref[q] = blocks(2 * q + mine)
        message[q * size : (q + 1) * size, :] = blocks(2 * q + 1 - mine)


def join_kernel(bit, ra_ref, rb_ref, la_ref, lb_ref, keep_ref, message, held):
    n, size, width = held.shape
    rows = size - 8
    count = la_ref.shape[0] // n
    thin = la_ref.shape[1]
    held[:, :rows, :] = (ra_ref[...] + rb_ref[...]).reshape(n, rows, width)
    held[:, rows:, :] = jnp.zeros((n, 8, width), F32)
    left = la_ref[...] + lb_ref[...]
    for q in range(n):
        held[q, rows : rows + count, :thin] = left[q * count : (q + 1) * count, :]
    write_split(bit, lambda q: held[q], keep_ref, message)


def join(bit, n, ra, rb, la, lb):
    rows, width = ra.shape
    size = rows // n + 8
    return pl.pallas_call(
        functools.partial(join_kernel, bit),
        in_specs=[VMEM] * 4,
        out_specs=[VMEM] * 2,
        out_shape=[
            sds((n // 2, size, width), F32),
            sds((n // 2 * size, width), F32),
        ],
        scratch_shapes=[pltpu.VMEM((n, size, width), F32)],
        compiler_params=params(8),
        cost_estimate=cost(rows * width, 8 * rows * width),
        name="join",
    )(ra, rb, la, lb)


def fold_kernel(bit, keep_ref, small_ref, came, *rest):
    next_keep, next_small, message = rest[-3:]
    parts, size, _ = keep_ref.shape
    write_split(
        bit,
        lambda q: keep_ref[q] + came[pl.ds(pl.multiple_of(q * size, 8), size), :],
        next_keep,
        message,
    )
    other = came[parts * size :, :] if len(rest) == 3 else rest[0][...]
    small = small_ref[...] + other
    next_small[...] = small
    message[parts // 2 * size :, :] = small


def fold(bit, keep, small, *came):
    parts, size, width = keep.shape
    tail = small.shape[0]
    shapes = [
        sds((parts // 2, size, width), F32),
        sds((tail, width), F32),
        sds((parts // 2 * size + tail, width), F32),
    ]
    return pl.pallas_call(
        functools.partial(fold_kernel, bit),
        in_specs=[VMEM] * (2 + len(came)),
        out_specs=[VMEM] * 3,
        out_shape=shapes,
        compiler_params=params(8),
        cost_estimate=cost(parts * size * width, 8 * parts * size * width),
        name="fold",
    )(keep, small, *came)


def close_kernel(keep_ref, small_ref, came, ta_ref, tb_ref, right_ref, left_ref, twiddle_ref, *vectors):
    _, size, width = keep_ref.shape
    rows, count, thin = size - 8, *left_ref.shape
    right_ref[...] = keep_ref[0, :rows, :] + came[:rows, :]
    left_ref[...] = keep_ref[0, rows : rows + count, :thin] + came[rows : rows + count, :thin]
    small = small_ref[...] + came[size:, :]
    lines = vectors[0].shape[1] // width
    for i, out_ref in enumerate(vectors):
        for j in range(lines):
            at = i * lines + j
            out_ref[:, j * width : (j + 1) * width] = small[at : at + 1, :]
    for a in range(twiddle_ref.shape[0]):
        twiddle_ref[a : a + 1, :] = ta_ref[a, :1, :] + tb_ref[a, :1, :]


def close(keep, small, came, ta, tb, count, thin, chans):
    _, size, width = keep.shape
    return pl.pallas_call(
        close_kernel,
        in_specs=[VMEM] * 5,
        out_shape=[
            sds((size - 8, width), F32),
            sds((count, thin), F32),
            sds((ta.shape[0], ta.shape[2]), F32),
        ]
        + [sds((1, chans), F32)] * 3,
        compiler_params=params(8),
        cost_estimate=cost(size * width, 8 * size * width),
        name="close",
    )(keep, small, came, ta, tb)


def row_sums(x):
    high = x.astype(BF16)
    low = (x - high.astype(F32)).astype(BF16)
    ones = jnp.ones((x.shape[1], 128), BF16)
    sums = jnp.dot(high, ones, preferred_element_type=F32) + jnp.dot(
        low, ones, preferred_element_type=F32
    )
    return sums.T[:8, :]


def column(rows):
    return rows.T[:, :1]


def scale_of(sa_ref, sb_ref):
    return column(lax.rsqrt((sa_ref[...] + sb_ref[...]) / D + EPS))


def sigmoid(x):
    return 0.5 * jnp.tanh(0.5 * x) + 0.5


def squares_kernel(tok_ref, out_ref):
    x = tok_ref[...].astype(F32)
    out_ref[...] = row_sums(x * x)


def squares(tokens):
    rows, width = tokens.shape
    return pl.pallas_call(
        squares_kernel,
        grid=(rows // B,),
        in_specs=[pl.BlockSpec((B, width), lambda a: (a, 0))],
        out_specs=pl.BlockSpec((8, B), lambda a: (0, a)),
        out_shape=sds((8, rows), F32),
        compiler_params=params(),
        cost_estimate=cost(8 * rows * width, 2 * rows * width),
        name="squares",
    )(tokens)


def gate_kernel(n, tok_ref, cot_ref, sa_ref, sb_ref, gain_ref, slope_ref, bias_ref, *rest):
    nb_ref, outs, held = rest[0], rest[1 : 1 + n], rest[1 + n]
    size = B // n
    normed = tok_ref[...].astype(F32) * scale_of(sa_ref, sb_ref) * gain_ref[...]
    nb_ref[0] = normed.astype(BF16)
    gate = sigmoid(slope_ref[...] * normed + bias_ref[...])
    held[...] = (cot_ref[...].astype(F32) * gate).astype(BF16)
    for k, dest in enumerate(partners(n, 1)):
        outs[k][0] = held[pl.ds(pl.multiple_of(dest * size, size), size), :]


def gate_cotangent(n, tokens, cotangent, sa, sb, gain, slope, bias):
    rows, width = tokens.shape
    blocks = rows // B
    size = B // n
    tall = pl.BlockSpec((B, width), lambda a: (a, 0))
    row = pl.BlockSpec((8, B), lambda a: (0, a))
    vec = whole((1, width))
    result = pl.pallas_call(
        functools.partial(gate_kernel, n),
        grid=(blocks,),
        in_specs=[tall, tall, row, row, vec, vec, vec],
        out_specs=[pl.BlockSpec((1, B, width), lambda a: (a, 0, 0))]
        + [pl.BlockSpec((1, size, width), lambda a: (a, 0, 0))] * n,
        out_shape=[sds((blocks, B, width), BF16)] + [sds((blocks, size, width), BF16)] * n,
        scratch_shapes=[pltpu.VMEM((B, width), BF16)],
        compiler_params=params(),
        cost_estimate=cost(20 * rows * width, 8 * rows * width),
        name="gate_cotangent",
    )(tokens, cotangent, sa, sb, gain, slope, bias)
    return result[0], list(result[1:])


def twiddle_column(tw_ref, a):
    return column(jnp.broadcast_to(tw_ref[pl.ds(a, 1), :], (8, tw_ref.shape[1])))


def first_kernel(n, nb_ref, right_ref, tw_ref, *rest):
    first_ref, outs, held = rest[0], rest[1 : 1 + n], rest[1 + n]
    size = B // n
    first = jnp.dot(right_ref[...], nb_ref[0], preferred_element_type=F32)
    first_ref[0] = first
    held[...] = (first * twiddle_column(tw_ref, pl.program_id(0))).astype(BF16)
    for k, dest in enumerate(partners(n, 1)):
        outs[k][0] = held[pl.ds(pl.multiple_of(dest * size, size), size), :]


def first_factor(n, normed_b, right, twiddle):
    blocks, _, width = normed_b.shape
    size = B // n
    block = pl.BlockSpec((1, B, width), lambda a: (a, 0, 0))
    result = pl.pallas_call(
        functools.partial(first_kernel, n),
        grid=(blocks,),
        in_specs=[block, whole((B, B)), whole((blocks, B))],
        out_specs=[block] + [pl.BlockSpec((1, size, width), lambda a: (a, 0, 0))] * n,
        out_shape=[sds((blocks, B, width), F32)] + [sds((blocks, size, width), BF16)] * n,
        scratch_shapes=[pltpu.VMEM((B, width), BF16)],
        compiler_params=params(),
        cost_estimate=cost(2 * blocks * B * B * width, 8 * blocks * B * width),
        name="first_factor",
    )(normed_b, right, twiddle)
    return result[0], list(result[1:])


def group_of(n):
    return min(16, B // n)


def spread_matrix(rows, cols, group, offset, transposed):
    shape = (cols, rows) if transposed else (rows, cols)
    m = lax.broadcasted_iota(jnp.int32, shape, 1 if transposed else 0) + offset
    r = lax.broadcasted_iota(jnp.int32, shape, 0 if transposed else 1)
    inside = (m >= r * group) & (m < (r + 1) * group)
    return jnp.where(inside, 1.0, 0.0).astype(BF16)


def same_place(rows, cols, group, offset):
    m = lax.broadcasted_iota(jnp.int32, (rows, cols), 0) + offset
    q = lax.broadcasted_iota(jnp.int32, (rows, cols), 1)
    return lax.rem(m, group) == lax.rem(q, group)


def widen_kernel(group, left_ref, fore_ref, back_ref):
    step, total = fore_ref.shape
    outer = left_ref.shape[0]
    offset = pl.program_id(0) * step
    rows = spread_matrix(step, outer, group, offset, False)
    cols = spread_matrix(total, outer, group, 0, True)
    same = same_place(step, total, group, offset)
    left = left_ref[...]
    for source, out_ref in ((left, fore_ref), (left.astype(F32).T.astype(BF16), back_ref)):
        part = jnp.dot(rows, source, preferred_element_type=F32).astype(BF16)
        full = jnp.dot(part, cols, preferred_element_type=F32)
        out_ref[...] = jnp.where(same, full, 0.0).astype(BF16)


def widen(left, group):
    outer = left.shape[0]
    total = outer * group
    step = 256
    spec = pl.BlockSpec((step, total), lambda i: (i, 0))
    return pl.pallas_call(
        functools.partial(widen_kernel, group),
        grid=(total // step,),
        in_specs=[whole((outer, outer))],
        out_specs=[spec, spec],
        out_shape=[sds((total, total), BF16)] * 2,
        compiler_params=params(),
        cost_estimate=cost(4 * total * total * outer, 4 * total * total),
        name="widen",
    )(left)


def fetch(pairs_of_refs, sems):
    copies = [
        pltpu.make_async_copy(source, target, sems.at[i])
        for i, (source, target) in enumerate(pairs_of_refs)
    ]
    for copy in copies:
        copy.start()
    return copies


def group_copies(ins, held, group):
    n = len(ins)
    count, size, _ = ins[0].shape
    sources = partners(n, -1)
    return [
        (
            ins[k].at[:, pl.ds(g * group, group), :],
            held.at[g, pl.ds(sources[k] * count, count), :, :],
        )
        for g in range(size // group)
        for k in range(n)
    ]


def second_kernel(n, group, mat_ref, *rest):
    ins, outs, held, done, sems = rest[:n], rest[n : 2 * n], *rest[2 * n :]
    count, size, width = outs[0].shape
    groups = size // group
    dests = partners(n, 1)
    copies = fetch(group_copies(ins, held, group), sems)
    span = count * group
    step = min(256, width)
    for g in range(groups):
        for copy in copies[g * n : (g + 1) * n]:
            copy.wait()
        for c in range(width // step):
            part = slice(c * step, (c + 1) * step)
            flat = held[g, :, :, part].reshape(-1, step)
            done[g, :, part] = jnp.dot(
                mat_ref[...], flat, preferred_element_type=F32
            ).astype(BF16)
        for k in range(n):
            place = pl.ds(pl.multiple_of(dests[k] * span, span), span)
            outs[k][:, pl.ds(g * group, group), :] = done[g, place, :].reshape(count, group, width)


def second_factor(n, matrix, blocks, name):
    count, size, width = blocks[0].shape
    group = group_of(n)
    groups = size // group
    total = matrix.shape[0]
    return list(
        pl.pallas_call(
            functools.partial(second_kernel, n, group),
            in_specs=[VMEM] + [HBM] * n,
            out_shape=[sds((count, size, width), BF16)] * n,
            scratch_shapes=[
                pltpu.VMEM((groups, n * count, group, width), BF16),
                pltpu.VMEM((groups, total, width), BF16),
                pltpu.SemaphoreType.DMA((groups * n,)),
            ],
            compiler_params=params(),
            cost_estimate=cost(2 * total * total * width * groups, 8 * n * count * size * width),
            name=name,
        )(matrix, *in_hbm(blocks))
    )


def halves(rows, columns):
    nc = lax.axis_size("chan")
    if nc == 2:
        return [sds((rows, columns // 2), F32)] * 2
    return [sds((8, 128), F32), sds((rows, columns), F32)]


def store_halves(full, keep_ref, give_ref):
    if lax.axis_size("chan") == 2:
        keep_ref[...], give_ref[...] = chan_halves(full)
    else:
        keep_ref[...] = jnp.zeros_like(keep_ref)
        give_ref[...] = full


def left_kernel(n, group, *rest):
    cots, spreads, keep_ref, give_ref = rest[:n], rest[n : 2 * n], *rest[2 * n : 2 * n + 2]
    held_c, held_s, summed, sems = rest[2 * n + 2 :]
    groups, outer, _, width = held_c.shape
    dims = (((1,), (1,)), ((), ()))
    total = outer * group
    step = min(256, total)
    copies = fetch(group_copies(cots, held_c, group) + group_copies(spreads, held_s, group), sems)
    for copy in copies:
        copy.wait()
    for r in range(total // step):
        product = sum(
            lax.dot_general(
                held_c[g, r * step // group : (r + 1) * step // group].reshape(step, width),
                held_s[g].reshape(total, width),
                dims,
                preferred_element_type=F32,
            )
            for g in range(groups)
        )
        kept = jnp.where(same_place(step, total, group, 0), product, 0.0)
        lines = step // group
        summed[r * lines : (r + 1) * lines, :] = kept.reshape(lines, group, total).sum(axis=1)
    gather = spread_matrix(total, outer, group, 0, False).astype(F32)
    full = jnp.dot(
        summed[...], gather, preferred_element_type=F32, precision=lax.Precision.HIGHEST
    )
    store_halves(full, keep_ref, give_ref)


def left_gradient(n, cots, spreads):
    count, size, width = cots[0].shape
    group = group_of(n)
    outer = n * count
    total = outer * group
    groups = size // group
    scratch = pltpu.VMEM((groups, outer, group, width), BF16)
    return pl.pallas_call(
        functools.partial(left_kernel, n, group),
        in_specs=[HBM] * (2 * n),
        out_shape=halves(outer, outer),
        scratch_shapes=[
            scratch,
            scratch,
            pltpu.VMEM((outer, total), F32),
            pltpu.SemaphoreType.DMA((2 * groups * n,)),
        ],
        compiler_params=params(),
        cost_estimate=cost(2 * total * total * width * (size // group), 8 * n * count * size * width),
        name="left_gradient",
    )(*in_hbm(cots), *in_hbm(spreads))


def row_copies(ins, held):
    n = len(ins)
    size = ins[0].shape[1]
    return [
        (ins[k], held.at[:, pl.ds(pl.multiple_of(source * size, size), size), :])
        for k, source in enumerate(partners(n, -1))
    ]


def back_kernel(n, first_ref, nb_ref, right_ref, tw_ref, *rest):
    ins, (twg_ref, mm_ref, keep_ref, give_ref), (held, sems) = rest[:n], rest[n : n + 4], rest[n + 4 :]
    copies = fetch(row_copies(ins, held), sems)
    turned = right_ref[...].astype(F32).T.astype(BF16)
    for copy in copies:
        copy.wait()
    total = None
    for a in range(nb_ref.shape[0]):
        grad = held[a].astype(F32)
        twg_ref[a] = row_sums(grad * first_ref[a])
        first_grad = (grad * twiddle_column(tw_ref, a)).astype(BF16)
        mm_ref[a] = jnp.dot(turned, first_grad, preferred_element_type=F32)
        part = lax.dot_general(
            first_grad, nb_ref[a], (((1,), (1,)), ((), ())), preferred_element_type=F32
        )
        total = part if a == 0 else total + part
    store_halves(total, keep_ref, give_ref)


def back_first(n, blocks, first_mix, normed_b, right, twiddle):
    count, _, width = normed_b.shape
    return pl.pallas_call(
        functools.partial(back_kernel, n),
        in_specs=[VMEM] * 4 + [HBM] * n,
        out_specs=[VMEM] * 4,
        out_shape=[sds((count, 8, B), F32), sds((count, B, width), F32)] + halves(B, B),
        scratch_shapes=[pltpu.VMEM((count, B, width), BF16), pltpu.SemaphoreType.DMA((n,))],
        compiler_params=params(),
        cost_estimate=cost(4 * count * B * B * width, 12 * count * B * width),
        name="back_first",
    )(first_mix, normed_b, right, twiddle, *in_hbm(blocks))


def finish_kernel(n, tok_ref, cot_ref, sa_ref, sb_ref, gain_ref, slope_ref, bias_ref, mm_ref, *rest):
    ins, (mixed_ref, scaled_ref, inner_ref, sums_ref), (held, sems) = (
        rest[:n],
        rest[n : n + 4],
        rest[n + 4 :],
    )
    copies = fetch(row_copies(ins, held), sems)
    for copy in copies:
        copy.wait()
    scale = lax.rsqrt((sa_ref[...] + sb_ref[...]) / D + EPS)
    gains, slopes, biases = [], [], []
    for a in range(mm_ref.shape[0]):
        rows = slice(a * B, (a + 1) * B)
        second = held[a].astype(F32)
        wide = tok_ref[rows, :].astype(F32)
        unit = wide * column(scale[:, rows])
        normed = unit * gain_ref[...]
        gate = sigmoid(slope_ref[...] * normed + bias_ref[...])
        mixed_ref[rows, :] = (gate * second).astype(BF16)
        gate_grad = cot_ref[rows, :].astype(F32) * second * gate * (1.0 - gate)
        normed_grad = mm_ref[a] + gate_grad * slope_ref[...]
        scaled = normed_grad * gain_ref[...]
        scaled_ref[rows, :] = scaled
        inner_ref[:, rows] = row_sums(scaled * wide)
        gains.append(jnp.sum(normed_grad * unit, axis=0, keepdims=True))
        slopes.append(jnp.sum(gate_grad * normed, axis=0, keepdims=True))
        biases.append(jnp.sum(gate_grad, axis=0, keepdims=True))
    for i, terms in enumerate((gains, slopes, biases)):
        line = sum(terms)
        part = sums_ref.shape[1]
        lines = line.shape[1] // part
        for j in range(lines):
            at = i * lines + j
            sums_ref[at : at + 1, :] = line[:, j * part : (j + 1) * part]
    for at in range(3 * lines, sums_ref.shape[0]):
        sums_ref[at : at + 1, :] = jnp.zeros((1, part), F32)


def finish(n, blocks, tokens, cotangent, sa, sb, gain, slope, bias, mm, part):
    rows, width = tokens.shape
    return pl.pallas_call(
        functools.partial(finish_kernel, n),
        in_specs=[VMEM] * 8 + [HBM] * n,
        out_specs=[VMEM] * 4,
        out_shape=[sds((rows, width), BF16), sds((rows, width), F32), sds((8, rows), F32), sds((8, part), F32)],
        scratch_shapes=[pltpu.VMEM((rows // B, B, width), BF16), pltpu.SemaphoreType.DMA((n,))],
        compiler_params=params(),
        cost_estimate=cost(40 * rows * width, 16 * rows * width),
        name="finish",
    )(tokens, cotangent, sa, sb, gain, slope, bias, mm, *in_hbm(blocks))


def token_kernel(tok_ref, scaled_ref, sa_ref, sb_ref, ia_ref, ib_ref, out_ref):
    scale = lax.rsqrt((sa_ref[...] + sb_ref[...]) / D + EPS)
    inner = (ia_ref[...] + ib_ref[...]) * (scale * scale * scale) / D
    out_ref[...] = (
        column(scale) * scaled_ref[...] - tok_ref[...].astype(F32) * column(inner)
    ).astype(BF16)


def token_gradient(tokens, scaled, sa, sb, ia, ib):
    rows, width = tokens.shape
    tall = pl.BlockSpec((B, width), lambda a: (a, 0))
    row = pl.BlockSpec((8, B), lambda a: (0, a))
    return pl.pallas_call(
        token_kernel,
        grid=(rows // B,),
        in_specs=[tall, tall, row, row, row, row],
        out_specs=tall,
        out_shape=sds((rows, width), BF16),
        compiler_params=params(),
        cost_estimate=cost(5 * rows * width, 8 * rows * width),
        name="token_gradient",
    )(tokens, scaled, sa, sb, ia, ib)


def on_device(
    tokens, cotangent, norm_gain, gate_slope, gate_bias, right_factor, left_factor, twiddle
):
    n = lax.axis_size("seq")
    rows, width = tokens.shape
    gain, slope, bias = (v.reshape(1, width) for v in (norm_gain, gate_slope, gate_bias))
    sa, sb = chan_terms(squares(tokens))
    normed_b, cot_blocks = gate_cotangent(n, tokens, cotangent, sa, sb, gain, slope, bias)
    cot_cols = exchange(cot_blocks)
    right = chan_gather(right_factor)
    first_mix, spread_blocks = first_factor(n, normed_b, right, twiddle)
    spread_cols = exchange(spread_blocks)
    fore, back = widen(chan_gather(left_factor), group_of(n))

    cot_cols, spread_cols = after_part(cot_cols, spread_cols)
    grad_back = exchange(second_factor(n, back, cot_cols, "spread_grad"))
    spread_cols, grad_back = after_part(spread_cols, grad_back)
    mix_blocks = second_factor(n, fore, spread_cols, "second_mix")
    left_keep, left_give = left_gradient(n, cot_cols, spread_cols)
    la, lb = chan_joined(left_keep, left_give)
    left_give, mix_blocks = lax.optimization_barrier((left_give, mix_blocks))
    mix_back = exchange(mix_blocks)
    grad_back, mix_back = after_part(grad_back, mix_back, LAST)
    twiddle_rows, mm, right_keep, right_give = back_first(
        n, grad_back, first_mix, normed_b, right, twiddle
    )
    part = B // lax.axis_size("chan")
    steps = bits(n)
    right_give, twiddle_rows, _ = lax.optimization_barrier((right_give, twiddle_rows, mix_back))
    ra, rb = chan_joined(right_keep, right_give)
    keep, message = join(steps[0], n, ra, rb, la, lb)
    came = flipped(message, steps[0])
    mixed, scaled, inner, sums = finish(
        n, mix_back, tokens, cotangent, sa, sb, gain, slope, bias, mm, part
    )
    ia, ib = chan_terms(inner)
    sums_came = flipped(sums, steps[0])
    token_grad = token_gradient(tokens, scaled, sa, sb, ia, ib)
    keep, sums, message = fold(steps[1], keep, sums, came, sums_came)
    came = flipped(message, steps[1])
    token_grad, came = lax.optimization_barrier((token_grad, came))
    for bit in steps[2:]:
        keep, sums, message = fold(bit, keep, sums, came)
        came = flipped(message, bit)
    ta, tb = chan_terms(twiddle_rows)
    right_out, left_out, twiddle_grad, *vectors = close(
        keep, sums, came, ta, tb, la.shape[0] // n, la.shape[1], width
    )
    return (mixed, token_grad, right_out, left_out, twiddle_grad, *(v.reshape(-1) for v in vectors))


def solution(mesh):
    return jax.shard_map(
        on_device,
        mesh=mesh,
        in_specs=(
            P("seq", "chan"),
            P("seq", "chan"),
            P("chan"),
            P("chan"),
            P("chan"),
            P("chan", None),
            P("chan", None),
            P("seq", None),
        ),
        out_specs=(
            P("seq", "chan"),
            P("seq", "chan"),
            P("seq", "chan"),
            P("seq", "chan"),
            P("seq", None),
            P("chan"),
            P("chan"),
            P("chan"),
        ),
        check_vma=False,
    )
```

```python
import functools

import jax
import jax.numpy as jnp
from jax import lax
from jax.experimental import pallas as pl
from jax.experimental.pallas import tpu as pltpu
from jax.sharding import PartitionSpec as P

D = 1024
B = 512
EPS = 1e-05
LAG = 8
LAST = 6
SHARE = 1000

F32 = jnp.float32
BF16 = jnp.bfloat16


def sds(shape, dtype):
    return jax.ShapeDtypeStruct(shape, dtype)


def cost(flops, nbytes):
    return pl.CostEstimate(flops=int(flops) // SHARE, bytes_accessed=int(nbytes) // SHARE, transcendentals=0)


def params(mib=20):
    return pltpu.CompilerParams(vmem_limit_bytes=mib * 1024 * 1024)


def whole(shape):
    zeros = (0,) * len(shape)
    return pl.BlockSpec(shape, lambda *_: zeros)


HBM = pl.BlockSpec(memory_space=pltpu.HBM)
VMEM = pl.BlockSpec(memory_space=pltpu.VMEM)


def partners(n, sign):
    me = lax.axis_index("seq")
    hi, lo = me // 4, me % 4
    high = n // 4
    lo_of = [lo, lo + 1 - 2 * (lo % 2), (lo + 2) % 4, 3 - lo]
    return [
        ((hi + (sign * (k // 4)) % high) % high) * 4 + lo_of[k % 4]
        for k in range(n)
    ]


def pairs(n, k):
    high = n // 4
    return [
        (i, ((i // 4 + k // 4) % high) * 4 + ((i % 4) ^ (k % 4)))
        for i in range(n)
    ]


def send_order(n):
    if n == 16:
        return [1, 8, 4, 12, 2, 9, 5, 13, 3, 10, 6, 14, 7, 11, 15]
    high = n // 4
    far_first = sorted(range(1, high), key=lambda d: (abs(d - high / 2), d))
    order = []
    for dl in range(4):
        order += [4 * dh + dl for dh in far_first]
        if dl < 3:
            order.append(dl + 1)
    return order


def exchange(blocks):
    n = len(blocks)
    out = list(blocks)
    for k in send_order(n):
        out[k] = lax.ppermute(blocks[k], "seq", pairs(n, k))
    return out


def in_hbm(blocks):
    return [pltpu.with_memory_space_constraint(x, pltpu.HBM) for x in blocks]


def after_part(values, started, count=LAG):
    keys = send_order(len(started))[:count]
    values, held = lax.optimization_barrier((values, [started[k] for k in keys]))
    started = list(started)
    for k, v in zip(keys, held):
        started[k] = v
    return values, started


def chan_terms(x):
    nc = lax.axis_size("chan")
    if nc == 2:
        return x, lax.ppermute(x, "chan", [(0, 1), (1, 0)])
    return lax.psum(x, "chan"), jnp.zeros_like(x)


def chan_gather(x):
    nc = lax.axis_size("chan")
    if nc != 2:
        return lax.all_gather(x, "chan", axis=0, tiled=True)
    other = lax.ppermute(x, "chan", [(0, 1), (1, 0)])
    first = lax.axis_index("chan") == 0
    return jnp.concatenate(
        [jnp.where(first, x, other), jnp.where(first, other, x)], axis=0
    )


def chan_halves(x):
    half = x.shape[1] // 2
    first = lax.axis_index("chan") == 0
    low, high = x[:, :half], x[:, half:]
    return jnp.where(first, low, high), jnp.where(first, high, low)


def chan_joined(keep, give):
    if lax.axis_size("chan") == 2:
        return keep, lax.ppermute(give, "chan", [(0, 1), (1, 0)])
    out = lax.psum_scatter(give, "chan", scatter_dimension=1, tiled=True)
    return out, jnp.zeros_like(out)


def flipped(x, bit):
    n = lax.axis_size("seq")
    return lax.ppermute(x, "seq", [(i, i ^ bit) for i in range(n)])


def bits(n):
    return [1 << i for i in range(n.bit_length() - 1)]


def write_split(bit, blocks, keep_ref, message):
    mine = (lax.axis_index("seq") // bit) % 2
    size = keep_ref.shape[1]
    for q in range(keep_ref.shape[0]):
        keep_ref[q] = blocks(2 * q + mine)
        message[q * size : (q + 1) * size, :] = blocks(2 * q + 1 - mine)


def join_kernel(bit, ra_ref, rb_ref, la_ref, lb_ref, keep_ref, message, held):
    n, size, width = held.shape
    rows = size - 8
    count = la_ref.shape[0] // n
    thin = la_ref.shape[1]
    held[:, :rows, :] = (ra_ref[...] + rb_ref[...]).reshape(n, rows, width)
    held[:, rows:, :] = jnp.zeros((n, 8, width), F32)
    left = la_ref[...] + lb_ref[...]
    for q in range(n):
        held[q, rows : rows + count, :thin] = left[q * count : (q + 1) * count, :]
    write_split(bit, lambda q: held[q], keep_ref, message)


def join(bit, n, ra, rb, la, lb):
    rows, width = ra.shape
    size = rows // n + 8
    return pl.pallas_call(
        functools.partial(join_kernel, bit),
        in_specs=[VMEM] * 4,
        out_specs=[VMEM] * 2,
        out_shape=[
            sds((n // 2, size, width), F32),
            sds((n // 2 * size, width), F32),
        ],
        scratch_shapes=[pltpu.VMEM((n, size, width), F32)],
        compiler_params=params(8),
        cost_estimate=cost(rows * width, 8 * rows * width),
        name="join",
    )(ra, rb, la, lb)


def fold_kernel(bit, keep_ref, small_ref, came, *rest):
    next_keep, next_small, message = rest[-3:]
    parts, size, _ = keep_ref.shape
    write_split(
        bit,
        lambda q: keep_ref[q] + came[pl.ds(pl.multiple_of(q * size, 8), size), :],
        next_keep,
        message,
    )
    other = came[parts * size :, :] if len(rest) == 3 else rest[0][...]
    small = small_ref[...] + other
    next_small[...] = small
    message[parts // 2 * size :, :] = small


def fold(bit, keep, small, *came):
    parts, size, width = keep.shape
    tail = small.shape[0]
    shapes = [
        sds((parts // 2, size, width), F32),
        sds((tail, width), F32),
        sds((parts // 2 * size + tail, width), F32),
    ]
    return pl.pallas_call(
        functools.partial(fold_kernel, bit),
        in_specs=[VMEM] * (2 + len(came)),
        out_specs=[VMEM] * 3,
        out_shape=shapes,
        compiler_params=params(8),
        cost_estimate=cost(parts * size * width, 8 * parts * size * width),
        name="fold",
    )(keep, small, *came)


def close_kernel(keep_ref, small_ref, came, ta_ref, tb_ref, right_ref, left_ref, twiddle_ref, *vectors):
    _, size, width = keep_ref.shape
    rows, count, thin = size - 8, *left_ref.shape
    right_ref[...] = keep_ref[0, :rows, :] + came[:rows, :]
    left_ref[...] = keep_ref[0, rows : rows + count, :thin] + came[rows : rows + count, :thin]
    small = small_ref[...] + came[size:, :]
    lines = vectors[0].shape[1] // width
    for i, out_ref in enumerate(vectors):
        for j in range(lines):
            at = i * lines + j
            out_ref[:, j * width : (j + 1) * width] = small[at : at + 1, :]
    for a in range(twiddle_ref.shape[0]):
        twiddle_ref[a : a + 1, :] = ta_ref[a, :1, :] + tb_ref[a, :1, :]


def close(keep, small, came, ta, tb, count, thin, chans):
    _, size, width = keep.shape
    return pl.pallas_call(
        close_kernel,
        in_specs=[VMEM] * 5,
        out_shape=[
            sds((size - 8, width), F32),
            sds((count, thin), F32),
            sds((ta.shape[0], ta.shape[2]), F32),
        ]
        + [sds((1, chans), F32)] * 3,
        compiler_params=params(8),
        cost_estimate=cost(size * width, 8 * size * width),
        name="close",
    )(keep, small, came, ta, tb)


def row_sums(x):
    high = x.astype(BF16)
    low = (x - high.astype(F32)).astype(BF16)
    ones = jnp.ones((x.shape[1], 128), BF16)
    sums = jnp.dot(high, ones, preferred_element_type=F32) + jnp.dot(
        low, ones, preferred_element_type=F32
    )
    return sums.T[:8, :]


def column(rows):
    return rows.T[:, :1]


def scale_of(sa_ref, sb_ref):
    return column(lax.rsqrt((sa_ref[...] + sb_ref[...]) / D + EPS))


def sigmoid(x):
    return 0.5 * jnp.tanh(0.5 * x) + 0.5


def squares_kernel(tok_ref, out_ref):
    x = tok_ref[...].astype(F32)
    out_ref[...] = row_sums(x * x)


def squares(tokens):
    rows, width = tokens.shape
    return pl.pallas_call(
        squares_kernel,
        grid=(rows // B,),
        in_specs=[pl.BlockSpec((B, width), lambda a: (a, 0))],
        out_specs=pl.BlockSpec((8, B), lambda a: (0, a)),
        out_shape=sds((8, rows), F32),
        compiler_params=params(),
        cost_estimate=cost(8 * rows * width, 2 * rows * width),
        name="squares",
    )(tokens)


def gate_kernel(n, tok_ref, cot_ref, sa_ref, sb_ref, gain_ref, slope_ref, bias_ref, *rest):
    nb_ref, outs, held = rest[0], rest[1 : 1 + n], rest[1 + n]
    size = B // n
    normed = tok_ref[...].astype(F32) * scale_of(sa_ref, sb_ref) * gain_ref[...]
    nb_ref[0] = normed.astype(BF16)
    gate = sigmoid(slope_ref[...] * normed + bias_ref[...])
    held[...] = (cot_ref[...].astype(F32) * gate).astype(BF16)
    for k, dest in enumerate(partners(n, 1)):
        outs[k][0] = held[pl.ds(pl.multiple_of(dest * size, size), size), :]


def gate_cotangent(n, tokens, cotangent, sa, sb, gain, slope, bias):
    rows, width = tokens.shape
    blocks = rows // B
    size = B // n
    tall = pl.BlockSpec((B, width), lambda a: (a, 0))
    row = pl.BlockSpec((8, B), lambda a: (0, a))
    vec = whole((1, width))
    result = pl.pallas_call(
        functools.partial(gate_kernel, n),
        grid=(blocks,),
        in_specs=[tall, tall, row, row, vec, vec, vec],
        out_specs=[pl.BlockSpec((1, B, width), lambda a: (a, 0, 0))]
        + [pl.BlockSpec((1, size, width), lambda a: (a, 0, 0))] * n,
        out_shape=[sds((blocks, B, width), BF16)] + [sds((blocks, size, width), BF16)] * n,
        scratch_shapes=[pltpu.VMEM((B, width), BF16)],
        compiler_params=params(),
        cost_estimate=cost(20 * rows * width, 8 * rows * width),
        name="gate_cotangent",
    )(tokens, cotangent, sa, sb, gain, slope, bias)
    return result[0], list(result[1:])


def twiddle_column(tw_ref, a):
    return column(jnp.broadcast_to(tw_ref[pl.ds(a, 1), :], (8, tw_ref.shape[1])))


def first_kernel(n, nb_ref, right_ref, tw_ref, *rest):
    first_ref, outs, held = rest[0], rest[1 : 1 + n], rest[1 + n]
    size = B // n
    first = jnp.dot(right_ref[...], nb_ref[0], preferred_element_type=F32)
    first_ref[0] = first
    held[...] = (first * twiddle_column(tw_ref, pl.program_id(0))).astype(BF16)
    for k, dest in enumerate(partners(n, 1)):
        outs[k][0] = held[pl.ds(pl.multiple_of(dest * size, size), size), :]


def first_factor(n, normed_b, right, twiddle):
    blocks, _, width = normed_b.shape
    size = B // n
    block = pl.BlockSpec((1, B, width), lambda a: (a, 0, 0))
    result = pl.pallas_call(
        functools.partial(first_kernel, n),
        grid=(blocks,),
        in_specs=[block, whole((B, B)), whole((blocks, B))],
        out_specs=[block] + [pl.BlockSpec((1, size, width), lambda a: (a, 0, 0))] * n,
        out_shape=[sds((blocks, B, width), F32)] + [sds((blocks, size, width), BF16)] * n,
        scratch_shapes=[pltpu.VMEM((B, width), BF16)],
        compiler_params=params(),
        cost_estimate=cost(2 * blocks * B * B * width, 8 * blocks * B * width),
        name="first_factor",
    )(normed_b, right, twiddle)
    return result[0], list(result[1:])


def group_of(n):
    return min(16, B // n)


def spread_matrix(rows, cols, group, offset, transposed):
    shape = (cols, rows) if transposed else (rows, cols)
    m = lax.broadcasted_iota(jnp.int32, shape, 1 if transposed else 0) + offset
    r = lax.broadcasted_iota(jnp.int32, shape, 0 if transposed else 1)
    inside = (m >= r * group) & (m < (r + 1) * group)
    return jnp.where(inside, 1.0, 0.0).astype(BF16)


def same_place(rows, cols, group, offset):
    m = lax.broadcasted_iota(jnp.int32, (rows, cols), 0) + offset
    q = lax.broadcasted_iota(jnp.int32, (rows, cols), 1)
    return lax.rem(m, group) == lax.rem(q, group)


def widen_kernel(group, left_ref, fore_ref, back_ref):
    step, total = fore_ref.shape
    outer = left_ref.shape[0]
    offset = pl.program_id(0) * step
    rows = spread_matrix(step, outer, group, offset, False)
    cols = spread_matrix(total, outer, group, 0, True)
    same = same_place(step, total, group, offset)
    left = left_ref[...]
    for source, out_ref in ((left, fore_ref), (left.astype(F32).T.astype(BF16), back_ref)):
        part = jnp.dot(rows, source, preferred_element_type=F32).astype(BF16)
        full = jnp.dot(part, cols, preferred_element_type=F32)
        out_ref[...] = jnp.where(same, full, 0.0).astype(BF16)


def widen(left, group):
    outer = left.shape[0]
    total = outer * group
    step = 256
    spec = pl.BlockSpec((step, total), lambda i: (i, 0))
    return pl.pallas_call(
        functools.partial(widen_kernel, group),
        grid=(total // step,),
        in_specs=[whole((outer, outer))],
        out_specs=[spec, spec],
        out_shape=[sds((total, total), BF16)] * 2,
        compiler_params=params(),
        cost_estimate=cost(4 * total * total * outer, 4 * total * total),
        name="widen",
    )(left)


def fetch(pairs_of_refs, sems):
    copies = [
        pltpu.make_async_copy(source, target, sems.at[i])
        for i, (source, target) in enumerate(pairs_of_refs)
    ]
    for copy in copies:
        copy.start()
    return copies


def group_copies(ins, held, group):
    n = len(ins)
    count, size, _ = ins[0].shape
    sources = partners(n, -1)
    return [
        (
            ins[k].at[:, pl.ds(g * group, group), :],
            held.at[g, pl.ds(sources[k] * count, count), :, :],
        )
        for g in range(size // group)
        for k in range(n)
    ]


def second_kernel(n, group, mat_ref, *rest):
    ins, outs, held, done, sems = rest[:n], rest[n : 2 * n], *rest[2 * n :]
    count, size, width = outs[0].shape
    groups = size // group
    dests = partners(n, 1)
    copies = fetch(group_copies(ins, held, group), sems)
    span = count * group
    step = min(256, width)
    for g in range(groups):
        for copy in copies[g * n : (g + 1) * n]:
            copy.wait()
        for c in range(width // step):
            part = slice(c * step, (c + 1) * step)
            flat = held[g, :, :, part].reshape(-1, step)
            done[g, :, part] = jnp.dot(
                mat_ref[...], flat, preferred_element_type=F32
            ).astype(BF16)
        for k in range(n):
            place = pl.ds(pl.multiple_of(dests[k] * span, span), span)
            outs[k][:, pl.ds(g * group, group), :] = done[g, place, :].reshape(count, group, width)


def second_factor(n, matrix, blocks, name):
    count, size, width = blocks[0].shape
    group = group_of(n)
    groups = size // group
    total = matrix.shape[0]
    return list(
        pl.pallas_call(
            functools.partial(second_kernel, n, group),
            in_specs=[VMEM] + [HBM] * n,
            out_shape=[sds((count, size, width), BF16)] * n,
            scratch_shapes=[
                pltpu.VMEM((groups, n * count, group, width), BF16),
                pltpu.VMEM((groups, total, width), BF16),
                pltpu.SemaphoreType.DMA((groups * n,)),
            ],
            compiler_params=params(),
            cost_estimate=cost(2 * total * total * width * groups, 8 * n * count * size * width),
            name=name,
        )(matrix, *in_hbm(blocks))
    )


def halves(rows, columns):
    nc = lax.axis_size("chan")
    if nc == 2:
        return [sds((rows, columns // 2), F32)] * 2
    return [sds((8, 128), F32), sds((rows, columns), F32)]


def store_halves(full, keep_ref, give_ref):
    if lax.axis_size("chan") == 2:
        keep_ref[...], give_ref[...] = chan_halves(full)
    else:
        keep_ref[...] = jnp.zeros_like(keep_ref)
        give_ref[...] = full


def left_kernel(n, group, *rest):
    cots, spreads, keep_ref, give_ref = rest[:n], rest[n : 2 * n], *rest[2 * n : 2 * n + 2]
    held_c, held_s, summed, sems = rest[2 * n + 2 :]
    groups, outer, _, width = held_c.shape
    dims = (((1,), (1,)), ((), ()))
    total = outer * group
    step = min(256, total)
    copies = fetch(group_copies(cots, held_c, group) + group_copies(spreads, held_s, group), sems)
    for copy in copies:
        copy.wait()
    for r in range(total // step):
        product = sum(
            lax.dot_general(
                held_c[g, r * step // group : (r + 1) * step // group].reshape(step, width),
                held_s[g].reshape(total, width),
                dims,
                preferred_element_type=F32,
            )
            for g in range(groups)
        )
        kept = jnp.where(same_place(step, total, group, 0), product, 0.0)
        lines = step // group
        summed[r * lines : (r + 1) * lines, :] = kept.reshape(lines, group, total).sum(axis=1)
    gather = spread_matrix(total, outer, group, 0, False).astype(F32)
    full = jnp.dot(
        summed[...], gather, preferred_element_type=F32, precision=lax.Precision.HIGHEST
    )
    store_halves(full, keep_ref, give_ref)


def left_gradient(n, cots, spreads):
    count, size, width = cots[0].shape
    group = group_of(n)
    outer = n * count
    total = outer * group
    groups = size // group
    scratch = pltpu.VMEM((groups, outer, group, width), BF16)
    return pl.pallas_call(
        functools.partial(left_kernel, n, group),
        in_specs=[HBM] * (2 * n),
        out_shape=halves(outer, outer),
        scratch_shapes=[
            scratch,
            scratch,
            pltpu.VMEM((outer, total), F32),
            pltpu.SemaphoreType.DMA((2 * groups * n,)),
        ],
        compiler_params=params(),
        cost_estimate=cost(2 * total * total * width * (size // group), 8 * n * count * size * width),
        name="left_gradient",
    )(*in_hbm(cots), *in_hbm(spreads))


def row_copies(ins, held):
    n = len(ins)
    size = ins[0].shape[1]
    return [
        (ins[k], held.at[:, pl.ds(pl.multiple_of(source * size, size), size), :])
        for k, source in enumerate(partners(n, -1))
    ]


def back_kernel(n, first_ref, nb_ref, right_ref, tw_ref, *rest):
    ins, (twg_ref, mm_ref, keep_ref, give_ref), (held, sems) = rest[:n], rest[n : n + 4], rest[n + 4 :]
    copies = fetch(row_copies(ins, held), sems)
    turned = right_ref[...].astype(F32).T.astype(BF16)
    for copy in copies:
        copy.wait()
    total = None
    for a in range(nb_ref.shape[0]):
        grad = held[a].astype(F32)
        twg_ref[a] = row_sums(grad * first_ref[a])
        first_grad = (grad * twiddle_column(tw_ref, a)).astype(BF16)
        mm_ref[a] = jnp.dot(turned, first_grad, preferred_element_type=F32)
        part = lax.dot_general(
            first_grad, nb_ref[a], (((1,), (1,)), ((), ())), preferred_element_type=F32
        )
        total = part if a == 0 else total + part
    store_halves(total, keep_ref, give_ref)


def back_first(n, blocks, first_mix, normed_b, right, twiddle):
    count, _, width = normed_b.shape
    return pl.pallas_call(
        functools.partial(back_kernel, n),
        in_specs=[VMEM] * 4 + [HBM] * n,
        out_specs=[VMEM] * 4,
        out_shape=[sds((count, 8, B), F32), sds((count, B, width), F32)] + halves(B, B),
        scratch_shapes=[pltpu.VMEM((count, B, width), BF16), pltpu.SemaphoreType.DMA((n,))],
        compiler_params=params(),
        cost_estimate=cost(4 * count * B * B * width, 12 * count * B * width),
        name="back_first",
    )(first_mix, normed_b, right, twiddle, *in_hbm(blocks))


def finish_kernel(n, tok_ref, cot_ref, sa_ref, sb_ref, gain_ref, slope_ref, bias_ref, mm_ref, *rest):
    ins, (mixed_ref, scaled_ref, inner_ref, sums_ref), (held, sems) = (
        rest[:n],
        rest[n : n + 4],
        rest[n + 4 :],
    )
    copies = fetch(row_copies(ins, held), sems)
    for copy in copies:
        copy.wait()
    scale = lax.rsqrt((sa_ref[...] + sb_ref[...]) / D + EPS)
    gains, slopes, biases = [], [], []
    for a in range(mm_ref.shape[0]):
        rows = slice(a * B, (a + 1) * B)
        second = held[a].astype(F32)
        wide = tok_ref[rows, :].astype(F32)
        unit = wide * column(scale[:, rows])
        normed = unit * gain_ref[...]
        gate = sigmoid(slope_ref[...] * normed + bias_ref[...])
        mixed_ref[rows, :] = (gate * second).astype(BF16)
        gate_grad = cot_ref[rows, :].astype(F32) * second * gate * (1.0 - gate)
        normed_grad = mm_ref[a] + gate_grad * slope_ref[...]
        scaled = normed_grad * gain_ref[...]
        scaled_ref[rows, :] = scaled
        inner_ref[:, rows] = row_sums(scaled * wide)
        gains.append(jnp.sum(normed_grad * unit, axis=0, keepdims=True))
        slopes.append(jnp.sum(gate_grad * normed, axis=0, keepdims=True))
        biases.append(jnp.sum(gate_grad, axis=0, keepdims=True))
    for i, terms in enumerate((gains, slopes, biases)):
        line = sum(terms)
        part = sums_ref.shape[1]
        lines = line.shape[1] // part
        for j in range(lines):
            at = i * lines + j
            sums_ref[at : at + 1, :] = line[:, j * part : (j + 1) * part]
    for at in range(3 * lines, sums_ref.shape[0]):
        sums_ref[at : at + 1, :] = jnp.zeros((1, part), F32)


def finish(n, blocks, tokens, cotangent, sa, sb, gain, slope, bias, mm, part):
    rows, width = tokens.shape
    return pl.pallas_call(
        functools.partial(finish_kernel, n),
        in_specs=[VMEM] * 8 + [HBM] * n,
        out_specs=[VMEM] * 4,
        out_shape=[sds((rows, width), BF16), sds((rows, width), F32), sds((8, rows), F32), sds((8, part), F32)],
        scratch_shapes=[pltpu.VMEM((rows // B, B, width), BF16), pltpu.SemaphoreType.DMA((n,))],
        compiler_params=params(),
        cost_estimate=cost(40 * rows * width, 16 * rows * width),
        name="finish",
    )(tokens, cotangent, sa, sb, gain, slope, bias, mm, *in_hbm(blocks))


def token_kernel(tok_ref, scaled_ref, sa_ref, sb_ref, ia_ref, ib_ref, out_ref):
    scale = lax.rsqrt((sa_ref[...] + sb_ref[...]) / D + EPS)
    inner = (ia_ref[...] + ib_ref[...]) * (scale * scale * scale) / D
    out_ref[...] = (
        column(scale) * scaled_ref[...] - tok_ref[...].astype(F32) * column(inner)
    ).astype(BF16)


def token_gradient(tokens, scaled, sa, sb, ia, ib):
    rows, width = tokens.shape
    tall = pl.BlockSpec((B, width), lambda a: (a, 0))
    row = pl.BlockSpec((8, B), lambda a: (0, a))
    return pl.pallas_call(
        token_kernel,
        grid=(rows // B,),
        in_specs=[tall, tall, row, row, row, row],
        out_specs=tall,
        out_shape=sds((rows, width), BF16),
        compiler_params=params(),
        cost_estimate=cost(5 * rows * width, 8 * rows * width),
        name="token_gradient",
    )(tokens, scaled, sa, sb, ia, ib)


def on_device(
    tokens, cotangent, norm_gain, gate_slope, gate_bias, right_factor, left_factor, twiddle
):
    n = lax.axis_size("seq")
    rows, width = tokens.shape
    gain, slope, bias = (v.reshape(1, width) for v in (norm_gain, gate_slope, gate_bias))
    sa, sb = chan_terms(squares(tokens))
    normed_b, cot_blocks = gate_cotangent(n, tokens, cotangent, sa, sb, gain, slope, bias)
    cot_cols = exchange(cot_blocks)
    right = chan_gather(right_factor)
    first_mix, spread_blocks = first_factor(n, normed_b, right, twiddle)
    spread_cols = exchange(spread_blocks)
    fore, back = widen(chan_gather(left_factor), group_of(n))

    cot_cols, spread_cols = after_part(cot_cols, spread_cols)
    grad_back = exchange(second_factor(n, back, cot_cols, "spread_grad"))
    spread_cols, grad_back = after_part(spread_cols, grad_back)
    mix_blocks = second_factor(n, fore, spread_cols, "second_mix")
    left_keep, left_give = left_gradient(n, cot_cols, spread_cols)
    la, lb = chan_joined(left_keep, left_give)
    left_give, mix_blocks = lax.optimization_barrier((left_give, mix_blocks))
    mix_back = exchange(mix_blocks)
    grad_back, mix_back = after_part(grad_back, mix_back, LAST)
    twiddle_rows, mm, right_keep, right_give = back_first(
        n, grad_back, first_mix, normed_b, right, twiddle
    )
    part = B // lax.axis_size("chan")
    steps = bits(n)
    right_give, twiddle_rows, _ = lax.optimization_barrier((right_give, twiddle_rows, mix_back))
    ra, rb = chan_joined(right_keep, right_give)
    keep, message = join(steps[0], n, ra, rb, la, lb)
    came = flipped(message, steps[0])
    mixed, scaled, inner, sums = finish(
        n, mix_back, tokens, cotangent, sa, sb, gain, slope, bias, mm, part
    )
    ia, ib = chan_terms(inner)
    sums_came = flipped(sums, steps[0])
    token_grad = token_gradient(tokens, scaled, sa, sb, ia, ib)
    keep, sums, message = fold(steps[1], keep, sums, came, sums_came)
    came = flipped(message, steps[1])
    token_grad, came = lax.optimization_barrier((token_grad, came))
    for bit in steps[2:]:
        keep, sums, message = fold(bit, keep, sums, came)
        came = flipped(message, bit)
    ta, tb = chan_terms(twiddle_rows)
    right_out, left_out, twiddle_grad, *vectors = close(
        keep, sums, came, ta, tb, la.shape[0] // n, la.shape[1], width
    )
    return (mixed, token_grad, right_out, left_out, twiddle_grad, *(v.reshape(-1) for v in vectors))


def solution(mesh):
    return jax.shard_map(
        on_device,
        mesh=mesh,
        in_specs=(
            P("seq", "chan"),
            P("seq", "chan"),
            P("chan"),
            P("chan"),
            P("chan"),
            P("chan", None),
            P("chan", None),
            P("seq", None),
        ),
        out_specs=(
            P("seq", "chan"),
            P("seq", "chan"),
            P("seq", "chan"),
            P("seq", "chan"),
            P("seq", None),
            P("chan"),
            P("chan"),
            P("chan"),
        ),
        check_vma=False,
    )
```
